32 devices in a mesh: pipe: 4 (over y, x), expert: 8 (over z, core).
Axes of the slice: x: 2, y: 2, z: 4, core: 2. Of those that a mesh axis runs over, the one named last changes fastest.
Arguments:
- x0: bfloat16 [2, 512, 3584], P(None, 'expert'), may hold values from -64 to 64
- cotangent: bfloat16 [2, 512, 3584], P(None, 'expert'), may hold values from -6 to 6
- expert_ids: int32 [4, 2, 512, 2], P('pipe', None, 'expert'), may hold values from 0 to 7, all different within a row; in each aligned block of 64 rows (0 to 63, 64 to 127, ..., all dimensions but the last counted through in order) at most 20 rows name the same one
- norm_gain: float32 [4, 3584], P('pipe'), may hold values from 0.1 to 1.9
- router: bfloat16 [4, 3584, 8], P('pipe'), may hold values from -0.09375 to 0.09375
- w_gate: bfloat16 [4, 8, 3584, 1024], P('pipe', 'expert'), may hold values from -0.09375 to 0.09375
- w_up: bfloat16 [4, 8, 3584, 1024], P('pipe', 'expert'), may hold values from -0.09375 to 0.09375
- w_down: bfloat16 [4, 8, 1024, 3584], P('pipe', 'expert'), may hold values from -0.1875 to 0.1875
Outputs:
- section_out: bfloat16 [4, 2, 512, 3584], P('pipe', None, 'expert')
- section_grad: bfloat16 [4, 2, 512, 3584], P('pipe', None, 'expert')
The draws below stay inside these ranges and needn't reach their ends.
Inputs may be any that keep to these rules, and one draw needn't show every extreme that they name: `expert_ids`: in every layer and micro-batch, the 64 rows of one index of expert name each expert at most 20 times, a bound that some block reaches in some of these blocks; the ids of a token differ.
All inputs are finite; a program needn't handle non-finite values.
Results may differ from the reference program's by a relative error of at most 0.029.
Values may be sent and summed in bfloat16 or wider, within the bound.
A program may use at most 128 MiB of HBM per device.

```python
import math
import jax
import jax.numpy as jnp
import numpy as np
from jax import lax

D = 3584
H = 1024
TOP_WIN = 2
MB = 2
TOK_DEV = 64
EXPERTS = 8
LAYERS = 4
TOKENS = 512
CAP = 20
N_EXPERT = 8


def draw_x0(key, part):
    key_base = jax.random.fold_in(key, 11)
    key_rows = jax.random.fold_in(key, 12)
    key_cols = jax.random.fold_in(key, 13)
    row_scale = jnp.exp(jax.random.uniform(key_rows, (MB, TOKENS, 1), jnp.float32, -1.15, 1.15))
    col_scale = jnp.exp(jax.random.uniform(key_cols, (1, 1, D), jnp.float32, -1.15, 1.15))
    values = jnp.clip(jax.random.normal(key_base, (MB, TOKENS, D), jnp.float32), -6.0, 6.0) * row_scale * col_scale
    return values.astype(jnp.bfloat16)


def level_of(own_key, dims, split, low, largest):
    def one(position, parts):
        draws = jax.random.uniform(jax.random.fold_in(jax.random.fold_in(own_key, 6), position), (parts,), jnp.float32, low / len(split), largest / len(split))
        return jnp.repeat(jnp.exp(draws), dims[position] // parts).reshape((-1,) + (1,) * (len(dims) - position - 1))

    loudness = one(*split[0])
    for cut in split[1:]:
        loudness = loudness * one(*cut)
    return loudness


def assign_block(key, own, number, rows, number_of, top, reach, skew):
    sequence = jax.random.permutation(key, number_of)
    packed, usual = load_shares(number_of, rows * top, reach, skew, True), load_shares(number_of, rows * top, reach, skew, False)
    places = jnp.arange(number_of)

    def named(tallies, offset_by):
        used = int((tallies > 0).sum())
        fixed = max(1, used // 4)
        moved = fixed + (places - fixed + offset_by * (used - fixed)) % max(1, number_of - fixed)
        return jnp.zeros((number_of,), jnp.int32).at[sequence[jnp.where(places < fixed, places, moved)]].set(jnp.asarray(tallies, jnp.int32))

    tallies = jnp.where(number % 4 == 0, named(packed, number // 4), named(usual, number - number // 4 - 1))
    mixed = jax.random.permutation(jax.random.fold_in(own, 3), number_of)
    source_of, sink = mixed[0:number_of // 2 * 2:2], mixed[1:number_of // 2 * 2:2]
    margin = jnp.minimum(tallies[source_of] - 1, reach - tallies[sink]) // 2
    margin = jnp.where((source_of == sequence[0]) | (sink == sequence[0]) | (tallies[sink] == 0), 0, jnp.maximum(margin, 0))
    moved = jax.random.randint(jax.random.fold_in(own, 4), (number_of // 2,), 0, 1 << 20) % (margin + 1)
    tallies = tallies.at[source_of].add(-moved).at[sink].add(moved)
    members = jnp.searchsorted(jnp.cumsum(tallies), jnp.arange(rows * top), side="right").astype(jnp.int32)
    listing = members.reshape(top, rows).T
    listing = listing[jax.random.permutation(jax.random.fold_in(own, 1), rows)]
    offset_by = jax.random.randint(jax.random.fold_in(own, 2), (rows, 1), 0, top)
    return jnp.take_along_axis(listing, (jnp.arange(top)[None, :] + offset_by) % top, axis=1)


def load_shares(amount, total, limit, skew, full):
    loads = [(1 << 20) // math.isqrt(standing ** skew) + 1 for standing in range(1, amount + 1)]
    largest = limit if full else min(limit, max(-(-total // amount), total * loads[0] // sum(loads)))
    least = 1 if total - largest >= amount - 1 else 0
    holding, surplus = [largest] + [least] * (amount - 1), total - largest - least * (amount - 1)
    while surplus > 0:
        candidates = [i for i in range(1, amount) if holding[i] < largest] or [i for i in range(1, amount) if holding[i] < limit]
        whole, budget = sum([loads[i] for i in candidates]), surplus
        for i in candidates:
            more = min(limit - holding[i], max(1, budget * loads[i] // whole), surplus)
            holding[i] = holding[i] + more
            surplus = surplus - more
    return np.array(holding)


def normal_values(key, dims, scale, limit, shards=(), kind=jnp.bfloat16):
    entries = scale * jax.random.normal(key, dims, jnp.float32)
    if shards:
        entries = entries * level_of(key, dims, shards, -0.22, 0.18)
    return jnp.clip(entries, -limit, limit).astype(kind)


def setup_inputs(seed: int = 0) -> dict:
    splits = jax.random.split(jax.random.key(seed), 9)
    x0 = draw_x0(jax.random.fold_in(splits[8], 71), 0)
    cotangent = normal_values(splits[1], (MB, TOKENS, D), 1.0, 6.0, ((1, 8),))
    expert_ids_keys = jax.random.split(jax.random.fold_in(splits[2], 1), LAYERS * MB * TOKENS // TOK_DEV)
    expert_ids_turns = jax.random.permutation(jax.random.fold_in(splits[2], 3), LAYERS * MB * TOKENS // TOK_DEV)
    expert_ids = jax.vmap(lambda own, number: assign_block(jax.random.fold_in(splits[2], 2), own, number, TOK_DEV, EXPERTS, TOP_WIN, CAP, 1))(expert_ids_keys, expert_ids_turns).reshape((LAYERS, MB, TOKENS, TOP_WIN))
    norm_gain = jnp.clip(1.0 + 0.18 * jax.random.normal(splits[3], (LAYERS, D), jnp.float32), 0.1, 1.9)
    router = normal_values(splits[4], (LAYERS, D, EXPERTS), D ** -0.5, 0.09375, ((0, 4),))
    w_gate = normal_values(splits[5], (LAYERS, EXPERTS, D, H), D ** -0.5, 0.09375, ((0, 4), (1, 8)))
    w_up = normal_values(splits[6], (LAYERS, EXPERTS, D, H), D ** -0.5, 0.09375, ((0, 4), (1, 8)))
    w_down = normal_values(splits[7], (LAYERS, EXPERTS, H, D), H ** -0.5, 0.1875, ((0, 4), (1, 8)))
    return {"x0": x0, "cotangent": cotangent, "expert_ids": expert_ids, "norm_gain": norm_gain, "router": router, "w_gate": w_gate, "w_up": w_up, "w_down": w_down}


EPS = 1e-06
ROUTE_SCALE = 2.5

def slot_table(route_ids, expert_count, capacity):
    hit_mask = (route_ids[:, None] == jnp.arange(expert_count, dtype=jnp.int32)[None, :]).astype(jnp.int32)
    before = jnp.cumsum(hit_mask, axis=0) - hit_mask
    place_idx = lax.optimization_barrier(jnp.sum(before * hit_mask, axis=1))
    target = route_ids * capacity + place_idx
    places = jnp.arange(expert_count * capacity, dtype=jnp.int32)
    return (places[:, None] == target[None, :]).astype(jnp.bfloat16)

def norm_gates(layer_in, norm_scale, router_w, route_ids, expert_count):
    values = layer_in.astype(jnp.float32)
    inv_rms = lax.rsqrt(lax.optimization_barrier(jnp.mean(values * values, axis=-1, keepdims=True)) + EPS)
    normed = (values * inv_rms * norm_scale).astype(jnp.bfloat16)
    logits = jnp.dot(normed, router_w, preferred_element_type=jnp.float32)
    pick_mask = (route_ids[:, :, None] == jnp.arange(expert_count, dtype=jnp.int32)[None, None, :]).astype(jnp.float32)
    chosen = lax.optimization_barrier(jnp.sum(pick_mask * logits[:, None, :], axis=-1))
    affinity = jax.nn.sigmoid(chosen)
    aff_total = lax.optimization_barrier(jnp.sum(affinity, axis=-1, keepdims=True))
    gate_vals = ROUTE_SCALE * affinity / aff_total
    return (inv_rms, normed, pick_mask, affinity, aff_total, gate_vals)

def expert_forward(row_block, gate_w, up_w, down_w):
    gate_proj = jnp.dot(row_block, gate_w, preferred_element_type=jnp.float32)
    up_proj = jnp.dot(row_block, up_w, preferred_element_type=jnp.float32)
    hidden_act = (jax.nn.silu(gate_proj) * up_proj).astype(jnp.bfloat16)
    result = jnp.dot(hidden_act, down_w, preferred_element_type=jnp.float32).astype(jnp.bfloat16)
    return (result, gate_proj, up_proj)

def expert_backward(grad_block, gate_proj, up_proj, gate_w, up_w, down_w):
    dhidden = jnp.dot(grad_block, down_w.T, preferred_element_type=jnp.float32)
    sigmoid_g = jax.nn.sigmoid(gate_proj)
    dgate_proj = (dhidden * up_proj * sigmoid_g * (1.0 + gate_proj * (1.0 - sigmoid_g))).astype(jnp.bfloat16)
    dup_proj = (dhidden * gate_proj * sigmoid_g).astype(jnp.bfloat16)
    summed = jnp.dot(dgate_proj, gate_w.T, preferred_element_type=jnp.float32) + jnp.dot(dup_proj, up_w.T, preferred_element_type=jnp.float32)
    return summed.astype(jnp.bfloat16)

def router_norm_grad(dgate_vals, grad_in, layer_in, inv_rms, norm_scale, router_w, pick_mask, affinity, aff_total, gate_vals, dnormed_experts):
    daff_vals = ROUTE_SCALE / aff_total * (dgate_vals - lax.optimization_barrier(jnp.sum(dgate_vals * gate_vals, axis=-1, keepdims=True)) / ROUTE_SCALE)
    dlogit = daff_vals * affinity * (1.0 - affinity)
    dlog_full = lax.optimization_barrier(jnp.sum(pick_mask * dlogit[:, :, None], axis=1))
    dnormed = dnormed_experts + jnp.dot(dlog_full, router_w.astype(jnp.float32).T, precision=lax.Precision.HIGHEST)
    values = layer_in.astype(jnp.float32)
    scaled_dn = dnormed * norm_scale
    inner_mean = lax.optimization_barrier(jnp.mean(scaled_dn * values, axis=-1, keepdims=True))
    result = grad_in.astype(jnp.float32) + inv_rms * scaled_dn - values * (inv_rms * inv_rms * inv_rms) * inner_mean
    return result.astype(jnp.bfloat16)

def to_blocks(tables, row_block):
    return jnp.einsum('bsr,brd->bsd', tables.astype(jnp.float32), row_block.astype(jnp.float32)).astype(jnp.bfloat16)

def from_blocks(tables, row_block):
    return jnp.einsum('bsr,bsd->brd', tables.astype(jnp.float32), row_block.astype(jnp.float32))

def swap_blocks(row_block):
    return row_block.reshape(N_EXPERT, N_EXPERT, CAP, D).transpose(1, 0, 2, 3).reshape(N_EXPERT, N_EXPERT * CAP, D)

def reference(x0, cotangent, expert_ids, norm_gain, router, w_gate, w_up, w_down):
    section_out = []
    forward_saved = []
    for layer_idx in range(LAYERS):
        outs_layer = []
        saved_layer = []
        for micro_idx in range(MB):
            layer_in = x0[micro_idx] if layer_idx == 0 else section_out[layer_idx - 1][micro_idx]
            route_ids = expert_ids[layer_idx, micro_idx]
            inv_rms, normed, pick_mask, affinity, aff_total, gate_vals = norm_gates(layer_in, norm_gain[layer_idx], router[layer_idx], route_ids, EXPERTS)
            tables = jax.vmap(lambda block_ids: slot_table(block_ids.reshape(-1), EXPERTS, CAP))(route_ids.reshape(N_EXPERT, TOK_DEV, TOP_WIN))
            send_tables = lax.optimization_barrier(jnp.sum(tables.reshape(N_EXPERT, EXPERTS * CAP, TOK_DEV, TOP_WIN), axis=3))
            expert_in = swap_blocks(to_blocks(send_tables, normed.reshape(N_EXPERT, TOK_DEV, D)))
            expert_out, gate_proj, up_proj = lax.map(lambda operands: expert_forward(operands[0], operands[1], operands[2], operands[3]), (expert_in, w_gate[layer_idx], w_up[layer_idx], w_down[layer_idx]))
            slot_vals = from_blocks(tables, swap_blocks(expert_out)).astype(jnp.bfloat16).reshape(TOKENS, TOP_WIN, D)
            mixed_rows = layer_in.astype(jnp.float32) + lax.optimization_barrier(jnp.sum(gate_vals[:, :, None] * slot_vals.astype(jnp.float32), axis=1))
            outs_layer.append(mixed_rows.astype(jnp.bfloat16))
            saved_layer.append((layer_in, inv_rms, pick_mask, affinity, aff_total, gate_vals, tables, gate_proj, up_proj, slot_vals))
        section_out.append(outs_layer)
        forward_saved.append(saved_layer)
    section_grad = [None] * LAYERS
    for layer_idx in reversed(range(LAYERS)):
        grads_layer = []
        for micro_idx in range(MB):
            grad_in = cotangent[micro_idx] if layer_idx == LAYERS - 1 else section_grad[layer_idx + 1][micro_idx]
            layer_in, inv_rms, pick_mask, affinity, aff_total, gate_vals, tables, gate_proj, up_proj, slot_vals = forward_saved[layer_idx][micro_idx]
            dgate_vals = lax.optimization_barrier(jnp.sum(grad_in.astype(jnp.float32)[:, None, :] * slot_vals.astype(jnp.float32), axis=-1))
            scaled = (gate_vals[:, :, None] * grad_in.astype(jnp.float32)[:, None, :]).astype(jnp.bfloat16)
            grad_rows = swap_blocks(to_blocks(tables, scaled.reshape(N_EXPERT, TOK_DEV * TOP_WIN, D)))
            expert_grad = lax.map(lambda operands: expert_backward(operands[0], operands[1], operands[2], operands[3], operands[4], operands[5]), (grad_rows, gate_proj, up_proj, w_gate[layer_idx], w_up[layer_idx], w_down[layer_idx]))
            slot_grads = from_blocks(tables, swap_blocks(expert_grad)).reshape(TOKENS, TOP_WIN, D)
            dnormed_experts = lax.optimization_barrier(jnp.sum(slot_grads, axis=1))
            grads_layer.append(router_norm_grad(dgate_vals, grad_in, layer_in, inv_rms, norm_gain[layer_idx], router[layer_idx], pick_mask, affinity, aff_total, gate_vals, dnormed_experts))
        section_grad[layer_idx] = grads_layer
    return (jnp.stack([jnp.stack(outs_layer) for outs_layer in section_out]), jnp.stack([jnp.stack(grads_layer) for grads_layer in section_grad]))
```

```python
import functools

import jax
import jax.numpy as jnp
from jax import lax
from jax.experimental import pallas as pl
from jax.experimental.pallas import tpu as pltpu
from jax.sharding import PartitionSpec as P

EPS = 1e-06
ROUTE_SCALE = 2.5
MESH = pl.DeviceIdType.MESH
F32 = jnp.float32
BF16 = jnp.bfloat16
PIECE = 512
HIGHEST = lax.Precision.HIGHEST
NEAR, FAR, BOTH = range(3)


def dot_nn(a, b):
    return jnp.dot(a, b, preferred_element_type=F32)


def dot_nt(a, b, precision=None):
    return lax.dot_general(
        a, b, (((1,), (1,)), ((), ())), preferred_element_type=F32, precision=precision
    )


def roles_of(count, first, second):
    odd = (count + 1) // 2 if count % 2 else count
    kinds = [first if i % 2 == 0 else second for i in range(count - count % 2)]
    return tuple(kinds[:odd] + [BOTH] * (count % 2) + kinds[odd:])


def split_of(capacity):
    extra = capacity - 16
    if extra in (1, 2, 4, 8):
        return 16, extra
    return -(-capacity // 8) * 8, 0


def stack(rows, parts):
    width = rows.shape[1] // parts
    return jnp.concatenate([rows[:, q * width : (q + 1) * width] for q in range(parts)], axis=0)


def unstack(rows, parts):
    height = rows.shape[0] // parts
    return jnp.concatenate([rows[q * height : (q + 1) * height] for q in range(parts)], axis=1)


def one_hot(rows_at, cols_at):
    return jnp.where(rows_at == cols_at, 1.0, 0.0).astype(BF16)


def kernel(
    sections,
    experts,
    cap,
    extra,
    x0_ref,
    cot_ref,
    gain_ref,
    router_ref,
    seat_row,
    seat_col,
    fold_row,
    fold_col,
    id_col,
    wg_hbm,
    wu_hbm,
    wd_hbm,
    out_ref,
    grad_ref,
    wg,
    wu,
    wd,
    xin,
    gin,
    send,
    recv,
    relay,
    row_send,
    row_recv,
    gproj,
    uproj,
    dhid,
    act_a,
    act_b,
    lhs,
    slots,
    base,
    stats,
    tab,
    tabt,
    ftab,
    ftabt,
    wsem,
    lsem,
    ssem,
    rsem,
    vssem,
    vrsem,
    fssem,
    frsem,
    pssem,
    prsem,
    tssem,
    trsem,
    tlsem,
):
    sec = lax.axis_index("pipe")
    me = lax.axis_index("expert")
    micro, toks, feat = x0_ref.shape
    hidden = wg.shape[1]
    top = seat_row.shape[1]
    places = experts * cap
    fold = 16 // extra if extra else 0
    count = feat // PIECE
    room = send.shape[3] // count
    ways = (roles_of(count, FAR, NEAR), roles_of(count, NEAR, FAR))
    relayed = [[c for c in range(count) if way[c] != NEAR] for way in ways]
    orders = (
        [c + 1 - 2 * (c % 2) if c < 4 else c for c in range(count)],
        list(range(count)),
    )
    half = feat // 2
    helper = lax.rem(sec + sections // 2, sections)
    hc = 512 if hidden % 512 == 0 else hidden
    inv_feat = 1.0 / feat
    parity = lax.rem(me, 2)
    others = pl.ds(0, (experts - 1) * cap)

    loads = [
        pltpu.make_async_copy(src, dst, wsem.at[i])
        for i, (src, dst) in enumerate(((wg_hbm, wg), (wu_hbm, wu), (wd_hbm, wd)))
    ]
    for load in loads:
        load.start()

    barrier = pltpu.get_barrier_semaphore()

    def greet(i, carry):
        pl.semaphore_signal(
            barrier, inc=1, device_id=(sec, lax.rem(me + i, experts)), device_id_type=MESH
        )
        return carry

    lax.fori_loop(1, experts, greet, 0)

    def greet_helper(i, carry):
        pl.semaphore_signal(barrier, inc=1, device_id=(helper, i), device_id_type=MESH)
        return carry

    lax.fori_loop(0, experts, greet_helper, 0)

    @pl.when(sec > 0)
    def _():
        pl.semaphore_signal(barrier, inc=1, device_id=(sec - 1, me), device_id_type=MESH)

    @pl.when(sec < sections - 1)
    def _():
        pl.semaphore_signal(barrier, inc=1, device_id=(sec + 1, me), device_id_type=MESH)

    neighbours = jnp.where(sec > 0, 1, 0) + jnp.where(sec < sections - 1, 1, 0)
    pl.semaphore_wait(barrier, 2 * experts - 1 + neighbours)

    def rows_of(e):
        return pl.ds(pl.multiple_of(e * cap, cap), cap)

    def cols(c, width):
        return pl.ds(pl.multiple_of(c * width, width), width)

    def piece(c):
        return pl.ds(c * PIECE, PIECE)

    def packed(c):
        return pl.ds(c * room, room)

    def relay_cols(p, c):
        return pl.ds(relayed[p % 2].index(c) * room, room)

    def each_other(body):
        def one(i, carry):
            body(lax.rem(me + i, experts))
            return carry

        lax.fori_loop(1, experts, one, 0)

    def slot_of(p, m):
        return p * micro + m

    def land_of(p, m):
        return (p % 2) * micro + m

    def direct(p, m, c, near, rows_src, rows_dst, peer):
        return pltpu.make_async_remote_copy(
            src_ref=send.at[p % 2, m, rows_src, packed(c)],
            dst_ref=recv.at[land_of(p, m), rows_dst, packed(c)],
            send_sem=(ssem if near else vssem).at[slot_of(p, m), c],
            recv_sem=(rsem if near else frsem).at[slot_of(p, m), c],
            device_id=(sec, peer),
            device_id_type=MESH,
        )

    def to_helper(p, m, c, peer):
        return pltpu.make_async_remote_copy(
            src_ref=send.at[p % 2, m, rows_of(peer), packed(c)],
            dst_ref=relay.at[slot_of(p, m), rows_of(peer), relay_cols(p, c)],
            send_sem=vssem.at[slot_of(p, m), c],
            recv_sem=vrsem.at[slot_of(p, m), relayed[p % 2].index(c), peer],
            device_id=(helper, me),
            device_id_type=MESH,
        )

    def from_helper(p, m, c, rows_src, rows_dst, mark):
        return pltpu.make_async_remote_copy(
            src_ref=relay.at[slot_of(p, m), rows_src, relay_cols(p, c)],
            dst_ref=recv.at[land_of(p, m), rows_dst, packed(c)],
            send_sem=fssem.at[slot_of(p, m), c],
            recv_sem=frsem.at[slot_of(p, m), c],
            device_id=(helper, mark),
            device_id_type=MESH,
        )

    def own_copy(p, m, c):
        return pltpu.make_async_copy(
            send.at[p % 2, m, rows_of(me), packed(c)],
            recv.at[land_of(p, m), rows_of(me), packed(c)],
            lsem.at[p % 2, m, c],
        )

    def start(p, m, c):
        way = ways[p % 2][c]

        def straight(peer):
            direct(p, m, c, True, rows_of(peer), rows_of(me), peer).start()

        def around(peer):
            same_chip = peer // 2 == me // 2

            @pl.when(same_chip)
            def _():
                direct(p, m, c, False, rows_of(peer), rows_of(me), peer).start()

            @pl.when(jnp.logical_not(same_chip))
            def _():
                to_helper(p, m, c, peer).start()

        def either(peer):
            alike = lax.rem(peer, 2) == parity

            @pl.when(alike)
            def _():
                straight(peer)

            @pl.when(jnp.logical_not(alike))
            def _():
                around(peer)

        each_other({NEAR: straight, FAR: around, BOTH: either}[way])
        own_copy(p, m, c).start()

    def arrive(p, m, c):
        own_copy(p, m, c).wait()
        other = lax.rem(me + 1, experts)
        for near, alone in ((True, NEAR), (False, FAR)):
            way = ways[p % 2][c]
            if way == BOTH:
                some = pl.ds(0, (experts // 2 - (1 if near else 0)) * cap)
                direct(p, m, c, near, some, some, other).wait()
            elif way == alone:
                direct(p, m, c, near, others, others, other).wait()

    def relay_pass(p, m):
        for c in relayed[p % 2]:
            both = ways[p % 2][c] == BOTH

            def one(mark):
                away = mark // 2 != me // 2
                if both:
                    away = jnp.logical_and(away, lax.rem(mark, 2) != parity)

                @pl.when(away)
                def _():
                    to_helper(p, m, c, mark).wait_recv()
                    from_helper(p, m, c, rows_of(mark), rows_of(me), mark).start()

            each_other(one)
        for c in relayed[p % 2]:
            both = ways[p % 2][c] == BOTH
            some = pl.ds(0, (experts // 2 - 1 if both else experts - 2) * cap)
            from_helper(p, m, c, some, some, lax.rem(me + 2, experts)).wait_send()

    def hop(src, dst, d, m, c, to):
        return pltpu.make_async_remote_copy(
            src_ref=src.at[m, :, piece(c)],
            dst_ref=dst.at[m, :, piece(c)],
            send_sem=pssem.at[d, m, c],
            recv_sem=prsem.at[d, m, c],
            device_id=(to, me),
            device_id_type=MESH,
        )

    def pair_of(ref, m):
        table = ref[m, 0]
        for k in range(1, top):
            table = table + ref[m, k]
        return table

    def make_tables():
        def at(shape, dim):
            return lax.broadcasted_iota(jnp.int32, shape, dim)

        for m in range(micro):
            for k in range(top):
                tab[m, k] = one_hot(at((places, toks), 0), seat_row[m, k])
                tabt[m, k] = one_hot(at((toks, places), 1), seat_col[m, k])
                if extra:
                    ftab[m, k] = one_hot(at((places, fold * toks), 0), fold_row[m, k])
                    ftabt[m, k] = one_hot(at((fold * toks, places), 1), fold_col[m, k])

    def folding(dim):
        low = extra.bit_length() - 1
        rows = (experts * extra).bit_length() - 1
        long = lax.broadcasted_iota(jnp.int32, (places, places), dim)
        short = lax.broadcasted_iota(jnp.int32, (places, places), 1 - dim)
        group = jnp.right_shift(long, rows)
        within = jnp.bitwise_and(long, (1 << rows) - 1)
        block = jnp.right_shift(within, low)
        return one_hot(block * cap + group * extra + jnp.bitwise_and(within, extra - 1), short)

    def unfolded(p, m, c):
        land = land_of(p, m)
        main = recv[land, :, pl.ds(c * room, PIECE)]
        if not extra:
            return main
        folded = recv[land, :, pl.ds(c * room + PIECE, room - PIECE)]
        more = unstack(dot_nn(folding(0), folded).astype(BF16), fold)
        return jnp.concatenate([main, more], axis=0)

    def put_results(m, c, result):
        send[1, m, :, pl.ds(c * room, PIECE)] = result[:places]
        if extra:
            send[1, m, :, pl.ds(c * room + PIECE, room - PIECE)] = dot_nn(
                folding(1), stack(result[places:], fold)
            ).astype(BF16)

    def put_rows(m, c, pairs):
        placed = functools.reduce(jnp.add, [dot_nn(main, rows) for main, _, rows in pairs])
        send[0, m, :, pl.ds(c * room, PIECE)] = placed.astype(BF16)
        if extra:
            placed = functools.reduce(
                jnp.add, [dot_nn(side, stack(rows, fold)) for _, side, rows in pairs]
            )
            send[0, m, :, pl.ds(c * room + PIECE, room - PIECE)] = placed.astype(BF16)

    def taken(p, m, c, main, side):
        land = land_of(p, m)
        rows = dot_nn(main, recv[land, :, pl.ds(c * room, PIECE)])
        if extra:
            folded = recv[land, :, pl.ds(c * room + PIECE, room - PIECE)]
            rows = rows + unstack(dot_nn(side, folded), fold)
        return rows

    def take(ref, whole, land, d, m, c, first, before):
        @pl.when(first)
        def _():
            land[m, :, piece(c)] = whole[m, :, piece(c)]

        @pl.when(jnp.logical_not(first))
        def _():
            hop(ref, land, d, m, c, before).wait_recv()

    def to_experts(m):
        main = pair_of(tab, m)
        side = pair_of(ftab, m) if extra else None
        for c in range(count):
            take(out_ref, x0_ref, xin, 0, m, c, sec == 0, sec - 1)
            put_rows(m, c, [(main, side, xin[m, :, piece(c)])])
            start(0, m, c)

    def pick(m, k):
        lanes = lax.broadcasted_iota(jnp.int32, (toks, experts), 1)
        return jnp.where(lanes == id_col[m, k], 1.0, 0.0)

    def gates_of(m):
        def square(c, acc):
            v = xin[m, :, cols(c, half)].astype(F32)
            return acc + jnp.sum(v * v, axis=-1, keepdims=True)

        total = lax.fori_loop(0, 2, square, jnp.zeros((toks, 1), F32))
        inv_rms = lax.rsqrt(total * inv_feat + EPS)

        def score(c, logits):
            at = cols(c, half)
            rows = (xin[m, :, at].astype(F32) * inv_rms * gain_ref[:, at]).astype(BF16)
            return logits + dot_nt(rows, router_ref[:, at])

        logits = lax.fori_loop(0, 2, score, jnp.zeros((toks, experts), F32))
        chosen = [jnp.sum(pick(m, k) * logits, axis=-1, keepdims=True) for k in range(top)]
        affinity = [jax.nn.sigmoid(c) for c in chosen]
        aff_total = functools.reduce(jnp.add, affinity)
        stats[m, 0] = inv_rms
        for k in range(top):
            stats[m, 2 + k] = affinity[k]
            stats[m, 2 + top + k] = ROUTE_SCALE * affinity[k] / aff_total
            stats[m, 2 + 2 * top + k] = chosen[k]

    def expert_up(m):
        total = jnp.zeros((lhs.shape[0], 1), F32)
        for c in orders[0]:
            at = piece(c)
            arrive(0, m, c)
            v = unfolded(0, m, c).astype(F32)
            total = total + jnp.sum(v * v, axis=-1, keepdims=True)
            lhs[...] = (v * gain_ref[:, at]).astype(BF16)
            opening = c == orders[0][0]

            def up(i, carry):
                hat = cols(i, hc)
                g = dot_nn(lhs[...], wg[at, hat])
                u = dot_nn(lhs[...], wu[at, hat])
                gproj[m, :, hat] = g if opening else gproj[m, :, hat] + g
                uproj[m, :, hat] = u if opening else uproj[m, :, hat] + u
                return carry

            lax.fori_loop(0, hidden // hc, up, 0)
        inv_rms = lax.rsqrt(total * inv_feat + EPS)

        def activate(c, carry):
            hat = cols(c, hc)
            g = gproj[m, :, hat] * inv_rms
            u = uproj[m, :, hat] * inv_rms
            gproj[m, :, hat] = g
            uproj[m, :, hat] = u
            act_a[:, hat] = (g * jax.nn.sigmoid(g) * u).astype(BF16)
            return carry

        lax.fori_loop(0, hidden // hc, activate, 0)

    def expert_down(m):
        for c in range(count):
            put_results(m, c, dot_nn(act_a[...], wd[:, piece(c)]).astype(BF16))
            start(1, m, c)

    def combine(m):
        gates = [stats[m, 2 + top + k] for k in range(top)]
        for c in orders[1]:
            at = piece(c)
            arrive(1, m, c)
            mixed = jnp.zeros((toks, PIECE), F32)
            for k in range(top):
                side = ftabt[m, k] if extra else None
                part = taken(1, m, c, tabt[m, k], side).astype(BF16)
                slots[m, k, :, at] = part
                mixed = mixed + gates[k] * part.astype(F32)
            out_ref[m, :, at] = (xin[m, :, at].astype(F32) + mixed).astype(BF16)

            @pl.when(sec < sections - 1)
            def _():
                hop(out_ref, xin, 0, m, c, sec + 1).start()

    def grads_to_experts(m):
        gates = [stats[m, 2 + top + k] for k in range(top)]
        for c in range(count):
            take(grad_ref, cot_ref, gin, 1, m, c, sec == sections - 1, sec + 1)
            dy = gin[m, :, piece(c)].astype(F32)
            put_rows(
                m,
                c,
                [
                    (tab[m, k], ftab[m, k] if extra else None, (gates[k] * dy).astype(BF16))
                    for k in range(top)
                ],
            )
            start(2, m, c)

    def router_grad(m):
        inv_rms = stats[m, 0]
        affinity = [stats[m, 2 + k] for k in range(top)]
        gates = [stats[m, 2 + top + k] for k in range(top)]
        aff_total = functools.reduce(jnp.add, affinity)

        def products(c, acc):
            at = cols(c, half)
            dy = gin[m, :, at].astype(F32)
            return tuple(
                acc[k] + jnp.sum(dy * slots[m, k, :, at].astype(F32), axis=-1, keepdims=True)
                for k in range(top)
            )

        dgates = lax.fori_loop(
            0, 2, products, tuple(jnp.zeros((toks, 1), F32) for _ in range(top))
        )
        inner = functools.reduce(jnp.add, [d * g for d, g in zip(dgates, gates)]) / ROUTE_SCALE
        dlog = jnp.zeros((toks, experts), F32)
        along = jnp.zeros((toks, 1), F32)
        for k in range(top):
            daff = ROUTE_SCALE / aff_total * (dgates[k] - inner)
            dlogit = daff * affinity[k] * (1.0 - affinity[k])
            dlog = dlog + pick(m, k) * dlogit
            along = along + dlogit * stats[m, 2 + 2 * top + k]
        stats[m, 1] = along

        def spread(c, carry):
            at = cols(c, half)
            term = jnp.dot(
                dlog,
                router_ref[:, at].astype(F32),
                preferred_element_type=F32,
                precision=HIGHEST,
            )
            base[m, :, at] = gin[m, :, at].astype(F32) + inv_rms * gain_ref[:, at] * term
            return carry

        lax.fori_loop(0, 2, spread, 0)

    def row_copy(m, rows_src, rows_dst, peer):
        return pltpu.make_async_remote_copy(
            src_ref=row_send.at[m, rows_src],
            dst_ref=row_recv.at[m, rows_dst],
            send_sem=tssem.at[m],
            recv_sem=trsem.at[m],
            device_id=(sec, peer),
            device_id_type=MESH,
        )

    def own_row(m):
        return pltpu.make_async_copy(
            row_send.at[m, rows_of(me)], row_recv.at[m, rows_of(me)], tlsem.at[m]
        )

    def expert_hidden_grad(m):
        for c in orders[0]:
            at = piece(c)
            arrive(2, m, c)
            lhs[...] = unfolded(2, m, c)
            opening = c == orders[0][0]

            def hidden_grad(i, carry):
                hat = cols(i, hc)
                d = dot_nt(lhs[...], wd[hat, at])
                dhid[:, hat] = d if opening else dhid[:, hat] + d
                return carry

            lax.fori_loop(0, hidden // hc, hidden_grad, 0)

        def activate(c, along):
            hat = cols(c, hc)
            dh = dhid[:, hat]
            g = gproj[m, :, hat]
            u = uproj[m, :, hat]
            s = jax.nn.sigmoid(g)
            a = (dh * u * s * (1.0 + g * (1.0 - s))).astype(BF16)
            b = (dh * g * s).astype(BF16)
            act_a[:, hat] = a
            act_b[:, hat] = b
            return along + jnp.sum(a.astype(F32) * g + b.astype(F32) * u, axis=-1, keepdims=True)

        along = jnp.zeros((lhs.shape[0], 1), F32)
        along = lax.fori_loop(0, hidden // hc, activate, along)
        message = jnp.broadcast_to(along[:places], row_send.shape[1:])
        if extra:
            few = jnp.broadcast_to(along[places:], (experts * extra, row_send.shape[2]))
            rest = jnp.zeros((places - experts * extra, row_send.shape[2]), F32)
            folded = jnp.dot(
                folding(1).astype(F32),
                jnp.concatenate([few, rest], axis=0),
                preferred_element_type=F32,
                precision=HIGHEST,
            )
            lanes = lax.broadcasted_iota(jnp.int32, row_send.shape[1:], 1)
            message = jnp.where(lanes == 0, message, folded)
        row_send[m] = message
        each_other(lambda peer: row_copy(m, rows_of(peer), rows_of(me), peer).start())
        own_row(m).start()

    def expert_rows_grad(m):
        for c in range(count):
            at = piece(c)
            summed = dot_nt(act_a[...], wg[at, :]) + dot_nt(act_b[...], wu[at, :])
            put_results(m, c, summed.astype(BF16))
            start(3, m, c)

    def row_sum(table, m):
        return jnp.dot(
            table.astype(F32), row_recv[m], preferred_element_type=F32, precision=HIGHEST
        )

    def gather(m):
        inv_rms = stats[m, 0]
        main = pair_of(tabt, m)
        side = pair_of(ftabt, m) if extra else None
        own_row(m).wait()
        row_copy(m, others, others, lax.rem(me + 1, experts)).wait()
        along = row_sum(main, m)[:, 0:1] + stats[m, 1]
        if extra:
            along = along + row_sum(side[:toks], m)[:, 1:2]
        scale_x = inv_rms * inv_rms * inv_feat * along
        for c in orders[1]:
            at = piece(c)
            arrive(3, m, c)
            dn = taken(3, m, c, main, side)
            grad_ref[m, :, at] = (
                base[m, :, at]
                + inv_rms * (gain_ref[:, at] * dn)
                - xin[m, :, at].astype(F32) * scale_x
            ).astype(BF16)

            @pl.when(sec > 0)
            def _():
                hop(grad_ref, gin, 1, m, c, sec - 1).start()

    def forward(m, carry):
        to_experts(m)
        gates_of(m)

        @pl.when(m > 0)
        def _():
            combine(m - 1)

        @pl.when(m == 0)
        def _():
            for load in loads:
                load.wait()

        expert_up(m)
        expert_down(m)
        return carry

    def backward(m, carry):
        grads_to_experts(m)
        router_grad(m)

        @pl.when(m > 0)
        def _():
            gather(m - 1)

        expert_hidden_grad(m)
        expert_rows_grad(m)
        return carry

    def relay_forward(m, carry):
        relay_pass(0, m)
        relay_pass(1, m)
        return carry

    def relay_backward(m, carry):
        relay_pass(2, m)
        relay_pass(3, m)
        return carry

    make_tables()
    early = sec < sections // 2

    @pl.when(jnp.logical_not(early))
    def _():
        lax.fori_loop(0, micro, relay_forward, 0)

    lax.fori_loop(0, micro, forward, 0)
    combine(micro - 1)

    @pl.when(early)
    def _():
        lax.fori_loop(0, micro, relay_forward, 0)
        lax.fori_loop(0, micro, relay_backward, 0)

    lax.fori_loop(0, micro, backward, 0)
    gather(micro - 1)

    @pl.when(jnp.logical_not(early))
    def _():
        lax.fori_loop(0, micro, relay_backward, 0)

    def drain(m, carry):
        @pl.when(sec < sections - 1)
        def _():
            for c in range(count):
                hop(out_ref, xin, 0, m, c, sec + 1).wait_send()

        @pl.when(sec > 0)
        def _():
            for c in range(count):
                hop(grad_ref, gin, 1, m, c, sec - 1).wait_send()

        return carry

    lax.fori_loop(0, micro, drain, 0)


def local(x0, cotangent, expert_ids, norm_gain, router, w_gate, w_up, w_down):
    sections = lax.axis_size("pipe")
    experts = lax.axis_size("expert")
    micro, toks, feat = x0.shape
    top = expert_ids.shape[3]
    cap, extra = split_of(toks * top * 5 // (4 * experts))
    fold = 16 // extra if extra else 0
    places = experts * cap
    every = places + experts * extra
    count = feat // PIECE
    room = PIECE + (PIECE // fold if extra else 0)
    ways = (roles_of(count, FAR, NEAR), roles_of(count, NEAR, FAR))
    relayed = max(sum(way != NEAR for way in ways_of) for ways_of in ways)
    hidden = w_gate.shape[3]
    ids = expert_ids[0]
    flat = ids.reshape(micro, toks * top)
    order = jnp.arange(toks * top, dtype=jnp.int32)
    earlier = (order[None, :] < order[:, None])[None]
    same = flat[:, :, None] == flat[:, None, :]
    place = jnp.sum(jnp.where(jnp.logical_and(same, earlier), 1, 0), axis=2)
    seat = jnp.where(place < cap, flat * cap + place, -1)
    seat = seat.reshape(micro, toks, top).transpose(0, 2, 1)
    ids = ids.transpose(0, 2, 1)
    if extra:
        quarter = jnp.arange(fold, dtype=jnp.int32)[None, :, None] * extra
        side = (flat * cap + place - cap)[:, None, :] + quarter
        side = jnp.where((place >= cap)[:, None, :], side, -1)
        side = side.reshape(micro, fold, toks, top).transpose(0, 3, 1, 2)
        side = side.reshape(micro, top, fold * toks)
    else:
        side = seat
    vmem = pl.BlockSpec(memory_space=pltpu.VMEM)
    hbm = pl.BlockSpec(memory_space=pl.ANY)
    out_rows, grad_rows = pl.pallas_call(
        functools.partial(kernel, sections, experts, cap, extra),
        out_shape=(jax.ShapeDtypeStruct(x0.shape, BF16), jax.ShapeDtypeStruct(x0.shape, BF16)),
        in_specs=[vmem] * 9 + [hbm] * 3,
        out_specs=(vmem, vmem),
        scratch_shapes=[
            pltpu.VMEM((feat, hidden), BF16),
            pltpu.VMEM((feat, hidden), BF16),
            pltpu.VMEM((hidden, feat), BF16),
            pltpu.VMEM((micro, toks, feat), BF16),
            pltpu.VMEM((micro, toks, feat), BF16),
            pltpu.VMEM((2, micro, places, count * room), BF16),
            pltpu.VMEM((2 * micro, places, count * room), BF16),
            pltpu.VMEM((4 * micro, places, relayed * room), BF16),
            pltpu.VMEM((micro, places, 128), F32),
            pltpu.VMEM((micro, places, 128), F32),
            pltpu.VMEM((micro, every, hidden), F32),
            pltpu.VMEM((micro, every, hidden), F32),
            pltpu.VMEM((every, hidden), F32),
            pltpu.VMEM((every, hidden), BF16),
            pltpu.VMEM((every, hidden), BF16),
            pltpu.VMEM((every, PIECE), BF16),
            pltpu.VMEM((micro, top, toks, feat), BF16),
            pltpu.VMEM((micro, toks, feat), F32),
            pltpu.VMEM((micro, 2 + 3 * top, toks, 1), F32),
            pltpu.VMEM((micro, top, places, toks), BF16),
            pltpu.VMEM((micro, top, toks, places), BF16),
            pltpu.VMEM((micro, top, places, side.shape[2]), BF16),
            pltpu.VMEM((micro, top, side.shape[2], places), BF16),
            pltpu.SemaphoreType.DMA((3,)),
            pltpu.SemaphoreType.DMA((2, micro, count)),
            pltpu.SemaphoreType.DMA((4 * micro, count)),
            pltpu.SemaphoreType.DMA((4 * micro, count)),
            pltpu.SemaphoreType.DMA((4 * micro, count)),
            pltpu.SemaphoreType.DMA((4 * micro, relayed, experts)),
            pltpu.SemaphoreType.DMA((4 * micro, count)),
            pltpu.SemaphoreType.DMA((4 * micro, count)),
            pltpu.SemaphoreType.DMA((2, micro, count)),
            pltpu.SemaphoreType.DMA((2, micro, count)),
            pltpu.SemaphoreType.DMA((micro,)),
            pltpu.SemaphoreType.DMA((micro,)),
            pltpu.SemaphoreType.DMA((micro,)),
        ],
        compiler_params=pltpu.CompilerParams(
            collective_id=0, has_side_effects=True, vmem_limit_bytes=62 * 1024 * 1024
        ),
    )(
        x0,
        cotangent,
        norm_gain,
        router[0].T,
        seat[:, :, None, :],
        seat[:, :, :, None],
        side[:, :, None, :],
        side[:, :, :, None],
        ids[:, :, :, None],
        w_gate[0, 0],
        w_up[0, 0],
        w_down[0, 0],
    )
    return (out_rows[None], grad_rows[None])


def solution(mesh):
    placed = (
        P(None, "expert", None),
        P(None, "expert", None),
        P("pipe", None, "expert", None),
        P("pipe", None),
        P("pipe", None, None),
        P("pipe", "expert", None, None),
        P("pipe", "expert", None, None),
        P("pipe", "expert", None, None),
    )
    return jax.shard_map(
        local,
        mesh=mesh,
        in_specs=placed,
        out_specs=(P("pipe", None, "expert", None), P("pipe", None, "expert", None)),
        check_vma=False,
    )
```

```python
import functools

import jax
import jax.numpy as jnp
from jax import lax
from jax.experimental import pallas as pl
from jax.experimental.pallas import tpu as pltpu
from jax.sharding import PartitionSpec as P

EPS = 1e-06
ROUTE_SCALE = 2.5
MESH = pl.DeviceIdType.MESH
F32 = jnp.float32
BF16 = jnp.bfloat16
PIECE = 512
LEAD = 3
HIGHEST = lax.Precision.HIGHEST
NEAR, FAR, BOTH = range(3)


def dot_nn(a, b):
    return jnp.dot(a, b, preferred_element_type=F32)


def dot_nt(a, b, precision=None):
    return lax.dot_general(
        a, b, (((1,), (1,)), ((), ())), preferred_element_type=F32, precision=precision
    )


def roles_of(count, all_both):
    if all_both:
        return (BOTH,) * (count - 1) + (NEAR,)
    return tuple(FAR if i % 2 else NEAR for i in range(count))


def split_of(capacity):
    extra = capacity - 16
    if extra in (1, 2, 4, 8):
        return 16, extra
    return -(-capacity // 8) * 8, 0


def stack(rows, parts):
    width = rows.shape[1] // parts
    return jnp.concatenate([rows[:, q * width : (q + 1) * width] for q in range(parts)], axis=0)


def unstack(rows, parts):
    height = rows.shape[0] // parts
    return jnp.concatenate([rows[q * height : (q + 1) * height] for q in range(parts)], axis=1)


def one_hot(rows_at, cols_at):
    return jnp.where(rows_at == cols_at, 1.0, 0.0).astype(BF16)


def kernel(
    sections,
    experts,
    cap,
    extra,
    x0_ref,
    cot_ref,
    gain_ref,
    router_ref,
    seat_row,
    seat_col,
    fold_row,
    fold_col,
    id_col,
    wg_hbm,
    wu_hbm,
    wd_hbm,
    out_ref,
    grad_ref,
    wg,
    wu,
    wd,
    xin,
    gin,
    send,
    recv,
    relay,
    row_send,
    row_recv,
    gproj,
    uproj,
    dhid,
    act_a,
    act_b,
    lhs,
    slots,
    base,
    stats,
    sums,
    scores,
    tab,
    tabt,
    ftab,
    ftabt,
    wsem,
    lsem,
    ssem,
    rsem,
    vssem,
    vrsem,
    fssem,
    frsem,
    pssem,
    prsem,
    tssem,
    trsem,
    tlsem,
):
    sec = lax.axis_index("pipe")
    me = lax.axis_index("expert")
    micro, toks, feat = x0_ref.shape
    hidden = wg.shape[1]
    top = seat_row.shape[1]
    places = experts * cap
    fold = 16 // extra if extra else 0
    count = feat // PIECE
    room = send.shape[3] // count
    ways = (roles_of(count, extra > 0),) * 2
    relayed = [[c for c in range(count) if way[c] != NEAR] for way in ways]
    orders = (list(range(count)), list(range(count)))
    half = feat // 2
    helper = lax.rem(sec + sections // 2, sections)
    hc = 512 if hidden % 512 == 0 else hidden
    inv_feat = 1.0 / feat
    parity = lax.rem(me, 2)
    others = pl.ds(0, (experts - 1) * cap)

    loads = [
        pltpu.make_async_copy(src, dst, wsem.at[i])
        for i, (src, dst) in enumerate(((wg_hbm, wg), (wu_hbm, wu), (wd_hbm, wd)))
    ]
    for load in loads:
        load.start()

    barrier = pltpu.get_barrier_semaphore()

    def greet(i, carry):
        pl.semaphore_signal(
            barrier, inc=1, device_id=(sec, lax.rem(me + i, experts)), device_id_type=MESH
        )
        return carry

    lax.fori_loop(1, experts, greet, 0)

    def greet_helper(i, carry):
        pl.semaphore_signal(barrier, inc=1, device_id=(helper, i), device_id_type=MESH)
        return carry

    lax.fori_loop(0, experts, greet_helper, 0)

    @pl.when(sec > 0)
    def _():
        pl.semaphore_signal(barrier, inc=1, device_id=(sec - 1, me), device_id_type=MESH)

    @pl.when(sec < sections - 1)
    def _():
        pl.semaphore_signal(barrier, inc=1, device_id=(sec + 1, me), device_id_type=MESH)

    neighbours = jnp.where(sec > 0, 1, 0) + jnp.where(sec < sections - 1, 1, 0)
    pl.semaphore_wait(barrier, 2 * experts - 1 + neighbours)

    def rows_of(e):
        return pl.ds(pl.multiple_of(e * cap, cap), cap)

    def cols(c, width):
        return pl.ds(pl.multiple_of(c * width, width), width)

    def piece(c):
        return pl.ds(c * PIECE, PIECE)

    def packed(c):
        return pl.ds(c * room, room)

    def relay_cols(p, c):
        return pl.ds(relayed[p % 2].index(c) * room, room)

    chips = experts // 2

    def each_other(body):
        body(2 * (me // 2) + 1 - parity, True, False)

        def chip(i, carry):
            there = 2 * lax.rem(me // 2 + i, chips)
            body(there + parity, False, True)
            body(there + 1 - parity, False, False)
            return carry

        if chips <= 4:
            for i in range(1, chips):
                chip(i, 0)
        else:
            lax.fori_loop(1, chips, chip, 0)

    def slot_of(p, m):
        return p * micro + m

    def land_of(p, m):
        return (p % 2) * micro + m

    def direct(p, m, c, near, rows_src, rows_dst, peer):
        return pltpu.make_async_remote_copy(
            src_ref=send.at[p % 2, m, rows_src, packed(c)],
            dst_ref=recv.at[land_of(p, m), rows_dst, packed(c)],
            send_sem=(ssem if near else vssem).at[slot_of(p, m), c],
            recv_sem=(rsem if near else frsem).at[slot_of(p, m), c],
            device_id=(sec, peer),
            device_id_type=MESH,
        )

    def to_helper(p, m, c, peer):
        return pltpu.make_async_remote_copy(
            src_ref=send.at[p % 2, m, rows_of(peer), packed(c)],
            dst_ref=relay.at[slot_of(p, m), rows_of(peer), relay_cols(p, c)],
            send_sem=vssem.at[slot_of(p, m), c],
            recv_sem=vrsem.at[slot_of(p, m), relayed[p % 2].index(c), peer],
            device_id=(helper, me),
            device_id_type=MESH,
        )

    def from_helper(p, m, c, rows_src, rows_dst, mark):
        return pltpu.make_async_remote_copy(
            src_ref=relay.at[slot_of(p, m), rows_src, relay_cols(p, c)],
            dst_ref=recv.at[land_of(p, m), rows_dst, packed(c)],
            send_sem=fssem.at[slot_of(p, m), c],
            recv_sem=frsem.at[slot_of(p, m), c],
            device_id=(helper, mark),
            device_id_type=MESH,
        )

    def own_copy(p, m, c):
        return pltpu.make_async_copy(
            send.at[p % 2, m, rows_of(me), packed(c)],
            recv.at[land_of(p, m), rows_of(me), packed(c)],
            lsem.at[p % 2, m, c],
        )

    def start(p, m, c):
        way = ways[p % 2][c]

        def one(peer, mate, alike):
            near = way == NEAR or (way == BOTH and alike)
            if near or mate:
                direct(p, m, c, near, rows_of(peer), rows_of(me), peer).start()
            else:
                to_helper(p, m, c, peer).start()

        each_other(one)
        own_copy(p, m, c).start()

    def arrive(p, m, c):
        own_copy(p, m, c).wait()
        other = lax.rem(me + 1, experts)
        for near, alone in ((True, NEAR), (False, FAR)):
            way = ways[p % 2][c]
            if way == BOTH:
                some = pl.ds(0, (experts // 2 - (1 if near else 0)) * cap)
                direct(p, m, c, near, some, some, other).wait()
            elif way == alone:
                direct(p, m, c, near, others, others, other).wait()

    def relay_pass(p, m):
        for c in relayed[p % 2]:
            both = ways[p % 2][c] == BOTH

            def one(mark, mate, alike):
                if not mate and not (both and alike):
                    to_helper(p, m, c, mark).wait_recv()
                    from_helper(p, m, c, rows_of(mark), rows_of(me), mark).start()

            each_other(one)
        for c in relayed[p % 2]:
            both = ways[p % 2][c] == BOTH
            some = pl.ds(0, (experts // 2 - 1 if both else experts - 2) * cap)
            from_helper(p, m, c, some, some, lax.rem(me + 2, experts)).wait_send()

    def hop(src, dst, d, m, c, to):
        return pltpu.make_async_remote_copy(
            src_ref=src.at[m, :, piece(c)],
            dst_ref=dst.at[m, :, piece(c)],
            send_sem=pssem.at[d, m, c],
            recv_sem=prsem.at[d, m, c],
            device_id=(to, me),
            device_id_type=MESH,
        )

    def pair_of(ref, m):
        table = ref[m, 0]
        for k in range(1, top):
            table = table + ref[m, k]
        return table

    def make_tables():
        def at(shape, dim):
            return lax.broadcasted_iota(jnp.int32, shape, dim)

        for m in range(micro):
            for k in range(top):
                tab[m, k] = one_hot(at((places, toks), 0), seat_row[m, k])
                tabt[m, k] = one_hot(at((toks, places), 1), seat_col[m, k])
                if extra:
                    ftab[m, k] = one_hot(at((places, fold * toks), 0), fold_row[m, k])
                    ftabt[m, k] = one_hot(at((fold * toks, places), 1), fold_col[m, k])

    def folding(dim):
        low = extra.bit_length() - 1
        rows = (experts * extra).bit_length() - 1
        long = lax.broadcasted_iota(jnp.int32, (places, places), dim)
        short = lax.broadcasted_iota(jnp.int32, (places, places), 1 - dim)
        group = jnp.right_shift(long, rows)
        within = jnp.bitwise_and(long, (1 << rows) - 1)
        block = jnp.right_shift(within, low)
        return one_hot(block * cap + group * extra + jnp.bitwise_and(within, extra - 1), short)

    def unfolded(p, m, c):
        land = land_of(p, m)
        main = recv[land, :, pl.ds(c * room, PIECE)]
        if not extra:
            return main
        folded = recv[land, :, pl.ds(c * room + PIECE, room - PIECE)]
        more = unstack(dot_nn(folding(0), folded).astype(BF16), fold)
        return jnp.concatenate([main, more], axis=0)

    def put_results(m, c, result):
        send[1, m, :, pl.ds(c * room, PIECE)] = result[:places]
        if extra:
            send[1, m, :, pl.ds(c * room + PIECE, room - PIECE)] = dot_nn(
                folding(1), stack(result[places:], fold)
            ).astype(BF16)

    def put_rows(m, c, pairs):
        placed = functools.reduce(jnp.add, [dot_nn(main, rows) for main, _, rows in pairs])
        send[0, m, :, pl.ds(c * room, PIECE)] = placed.astype(BF16)
        if extra:
            placed = functools.reduce(
                jnp.add, [dot_nn(side, stack(rows, fold)) for _, side, rows in pairs]
            )
            send[0, m, :, pl.ds(c * room + PIECE, room - PIECE)] = placed.astype(BF16)

    def taken(p, m, c, main, side):
        land = land_of(p, m)
        rows = dot_nn(main, recv[land, :, pl.ds(c * room, PIECE)])
        if extra:
            folded = recv[land, :, pl.ds(c * room + PIECE, room - PIECE)]
            rows = rows + unstack(dot_nn(side, folded), fold)
        return rows

    def take(ref, whole, land, d, m, c, first, before):
        @pl.when(first)
        def _():
            land[m, :, piece(c)] = whole[m, :, piece(c)]

        @pl.when(jnp.logical_not(first))
        def _():
            hop(ref, land, d, m, c, before).wait_recv()

    def pick(m, k):
        lanes = lax.broadcasted_iota(jnp.int32, (toks, experts), 1)
        return jnp.where(lanes == id_col[m, k], 1.0, 0.0)

    def gates_of(m):
        inv_rms = lax.rsqrt(sums[0] * inv_feat + EPS)
        logits = scores[...] * inv_rms
        chosen = [jnp.sum(pick(m, k) * logits, axis=-1, keepdims=True) for k in range(top)]
        affinity = [jax.nn.sigmoid(c) for c in chosen]
        aff_total = functools.reduce(jnp.add, affinity)
        stats[m, 0] = inv_rms
        for k in range(top):
            stats[m, 2 + k] = affinity[k]
            stats[m, 2 + top + k] = ROUTE_SCALE * affinity[k] / aff_total
            stats[m, 2 + 2 * top + k] = chosen[k]

    def to_experts(m, c):
        at = piece(c)
        main = pair_of(tab, m)
        side = pair_of(ftab, m) if extra else None
        take(out_ref, x0_ref, xin, 0, m, c, sec == 0, sec - 1)
        put_rows(m, c, [(main, side, xin[m, :, at])])
        start(0, m, c)
        v = xin[m, :, at].astype(F32)
        own = jnp.sum(v * v, axis=-1, keepdims=True)
        logits = dot_nt((v * gain_ref[:, at]).astype(BF16), router_ref[:, at])
        sums[0] = own if c == 0 else sums[0] + own
        scores[...] = logits if c == 0 else scores[...] + logits

    def expert_up(m):
        gates_of(m)
        total = jnp.zeros((lhs.shape[0], 1), F32)
        for c in orders[0]:
            at = piece(c)
            arrive(0, m, c)
            if c == orders[0][0] and m == 0:
                for load in loads:
                    load.wait()
            v = unfolded(0, m, c).astype(F32)
            total = total + jnp.sum(v * v, axis=-1, keepdims=True)
            lhs[...] = (v * gain_ref[:, at]).astype(BF16)
            g = dot_nn(lhs[...], wg[at, :])
            u = dot_nn(lhs[...], wu[at, :])
            opening = c == orders[0][0]
            gproj[m] = g if opening else gproj[m] + g
            uproj[m] = u if opening else uproj[m] + u
        inv_rms = lax.rsqrt(total * inv_feat + EPS)

        def activate(c, carry):
            hat = cols(c, hc)
            g = gproj[m, :, hat] * inv_rms
            u = uproj[m, :, hat] * inv_rms
            gproj[m, :, hat] = g
            uproj[m, :, hat] = u
            act_a[:, hat] = (g * jax.nn.sigmoid(g) * u).astype(BF16)
            return carry

        lax.fori_loop(0, hidden // hc, activate, 0)

    def expert_down(m):
        for c in range(count):
            put_results(m, c, dot_nn(act_a[...], wd[:, piece(c)]).astype(BF16))
            start(1, m, c)

    def combine(m, c):
        gates = [stats[m, 2 + top + k] for k in range(top)]
        at = piece(c)
        arrive(1, m, c)
        mixed = jnp.zeros((toks, PIECE), F32)
        for k in range(top):
            side = ftabt[m, k] if extra else None
            part = taken(1, m, c, tabt[m, k], side).astype(BF16)
            slots[m, k, :, at] = part
            mixed = mixed + gates[k] * part.astype(F32)
        out_ref[m, :, at] = (xin[m, :, at].astype(F32) + mixed).astype(BF16)

        @pl.when(sec < sections - 1)
        def _():
            hop(out_ref, xin, 0, m, c, sec + 1).start()

    def grads_to_experts(m, c):
        gates = [stats[m, 2 + top + k] for k in range(top)]
        at = piece(c)
        take(grad_ref, cot_ref, gin, 1, m, c, sec == sections - 1, sec + 1)
        dy = gin[m, :, at].astype(F32)
        put_rows(
            m,
            c,
            [
                (tab[m, k], ftab[m, k] if extra else None, (gates[k] * dy).astype(BF16))
                for k in range(top)
            ],
        )
        start(2, m, c)
        for k in range(top):
            own = jnp.sum(dy * slots[m, k, :, at].astype(F32), axis=-1, keepdims=True)
            sums[1 + k] = own if c == 0 else sums[1 + k] + own

    def expert_hidden_grad(m):
        router_grad(m)
        for c in orders[0]:
            arrive(2, m, c)
            lhs[...] = unfolded(2, m, c)
            d = dot_nt(lhs[...], wd[:, piece(c)])
            dhid[...] = d if c == orders[0][0] else dhid[...] + d
        hidden_done(m)

    def router_grad(m):
        inv_rms = stats[m, 0]
        affinity = [stats[m, 2 + k] for k in range(top)]
        gates = [stats[m, 2 + top + k] for k in range(top)]
        aff_total = functools.reduce(jnp.add, affinity)
        dgates = [sums[1 + k] for k in range(top)]
        inner = functools.reduce(jnp.add, [d * g for d, g in zip(dgates, gates)]) / ROUTE_SCALE
        dlog = jnp.zeros((toks, experts), F32)
        along = jnp.zeros((toks, 1), F32)
        for k in range(top):
            daff = ROUTE_SCALE / aff_total * (dgates[k] - inner)
            dlogit = daff * affinity[k] * (1.0 - affinity[k])
            dlog = dlog + pick(m, k) * dlogit
            along = along + dlogit * stats[m, 2 + 2 * top + k]
        stats[m, 1] = along

        def spread(c, carry):
            at = cols(c, half)
            term = jnp.dot(
                dlog,
                router_ref[:, at].astype(F32),
                preferred_element_type=F32,
                precision=HIGHEST,
            )
            base[m, :, at] = gin[m, :, at].astype(F32) + inv_rms * gain_ref[:, at] * term
            return carry

        lax.fori_loop(0, 2, spread, 0)

    def row_copy(m, rows_src, rows_dst, peer):
        return pltpu.make_async_remote_copy(
            src_ref=row_send.at[m, rows_src],
            dst_ref=row_recv.at[m, rows_dst],
            send_sem=tssem.at[m],
            recv_sem=trsem.at[m],
            device_id=(sec, peer),
            device_id_type=MESH,
        )

    def own_row(m):
        return pltpu.make_async_copy(
            row_send.at[m, rows_of(me)], row_recv.at[m, rows_of(me)], tlsem.at[m]
        )

    def hidden_done(m):
        def activate(c, along):
            hat = cols(c, hc)
            dh = dhid[:, hat]
            g = gproj[m, :, hat]
            u = uproj[m, :, hat]
            s = jax.nn.sigmoid(g)
            a = (dh * u * s * (1.0 + g * (1.0 - s))).astype(BF16)
            b = (dh * g * s).astype(BF16)
            act_a[:, hat] = a
            act_b[:, hat] = b
            return along + jnp.sum(a.astype(F32) * g + b.astype(F32) * u, axis=-1, keepdims=True)

        along = jnp.zeros((lhs.shape[0], 1), F32)
        along = lax.fori_loop(0, hidden // hc, activate, along)
        message = jnp.broadcast_to(along[:places], row_send.shape[1:])
        if extra:
            few = jnp.broadcast_to(along[places:], (experts * extra, row_send.shape[2]))
            rest = jnp.zeros((places - experts * extra, row_send.shape[2]), F32)
            folded = jnp.dot(
                folding(1).astype(F32),
                jnp.concatenate([few, rest], axis=0),
                preferred_element_type=F32,
                precision=HIGHEST,
            )
            lanes = lax.broadcasted_iota(jnp.int32, row_send.shape[1:], 1)
            message = jnp.where(lanes == 0, message, folded)
        row_send[m] = message
        each_other(lambda peer, mate, alike: row_copy(m, rows_of(peer), rows_of(me), peer).start())
        own_row(m).start()

    def row_sum(table, m):
        return jnp.dot(
            table.astype(F32), row_recv[m], preferred_element_type=F32, precision=HIGHEST
        )

    def expert_rows_grad(m):
        for c in range(count):
            at = piece(c)
            summed = dot_nt(act_a[...], wg[at, :]) + dot_nt(act_b[...], wu[at, :])
            put_results(m, c, summed.astype(BF16))
            start(3, m, c)

    def gather(m, c):
        inv_rms = stats[m, 0]
        at = piece(c)
        main = pair_of(tabt, m)
        side = pair_of(ftabt, m) if extra else None
        if c == 0:
            own_row(m).wait()
            row_copy(m, others, others, lax.rem(me + 1, experts)).wait()
            along = row_sum(main, m)[:, 0:1] + stats[m, 1]
            if extra:
                along = along + row_sum(side[:toks], m)[:, 1:2]
            stats[m, 1] = inv_rms * inv_rms * inv_feat * along
        arrive(3, m, c)
        dn = taken(3, m, c, main, side)
        grad_ref[m, :, at] = (
            base[m, :, at]
            + inv_rms * (gain_ref[:, at] * dn)
            - xin[m, :, at].astype(F32) * stats[m, 1]
        ).astype(BF16)

        @pl.when(sec > 0)
        def _():
            hop(grad_ref, gin, 1, m, c, sec - 1).start()

    def weave(inward, m, outward, before):
        for c in range(count + LEAD):
            if c >= LEAD:
                outward(before, c - LEAD)
            if c < count:
                inward(m, c)

    def in_turn(body, m):
        for c in range(count):
            body(m, c)

    def relay_forward(m, carry):
        relay_pass(0, m)
        relay_pass(1, m)
        return carry

    def relay_backward(m, carry):
        relay_pass(2, m)
        relay_pass(3, m)
        return carry

    make_tables()
    early = sec < sections // 2

    @pl.when(jnp.logical_not(early))
    def _():
        lax.fori_loop(0, micro, relay_forward, 0)

    for m in range(micro):
        if m == 0:
            in_turn(to_experts, m)
        else:
            weave(to_experts, m, combine, m - 1)
        expert_up(m)
        expert_down(m)

    @pl.when(sec == sections - 1)
    def _():
        weave(grads_to_experts, 0, combine, micro - 1)

    @pl.when(sec < sections - 1)
    def _():
        in_turn(combine, micro - 1)

        @pl.when(early)
        def _():
            lax.fori_loop(0, micro, relay_forward, 0)
            lax.fori_loop(0, micro, relay_backward, 0)

        in_turn(grads_to_experts, 0)

    for m in range(micro):
        if m > 0:
            weave(grads_to_experts, m, gather, m - 1)
        expert_hidden_grad(m)
        expert_rows_grad(m)
    in_turn(gather, micro - 1)

    @pl.when(jnp.logical_not(early))
    def _():
        lax.fori_loop(0, micro, relay_backward, 0)

    def drain(m, carry):
        @pl.when(sec < sections - 1)
        def _():
            for c in range(count):
                hop(out_ref, xin, 0, m, c, sec + 1).wait_send()

        @pl.when(sec > 0)
        def _():
            for c in range(count):
                hop(grad_ref, gin, 1, m, c, sec - 1).wait_send()

        return carry

    lax.fori_loop(0, micro, drain, 0)


def local(x0, cotangent, expert_ids, norm_gain, router, w_gate, w_up, w_down):
    sections = lax.axis_size("pipe")
    experts = lax.axis_size("expert")
    micro, toks, feat = x0.shape
    top = expert_ids.shape[3]
    cap, extra = split_of(toks * top * 5 // (4 * experts))
    fold = 16 // extra if extra else 0
    places = experts * cap
    every = places + experts * extra
    count = feat // PIECE
    room = PIECE + (PIECE // fold if extra else 0)
    relayed = sum(way != NEAR for way in roles_of(count, extra > 0))
    hidden = w_gate.shape[3]
    ids = expert_ids[0]
    flat = ids.reshape(micro, toks * top)
    order = jnp.arange(toks * top, dtype=jnp.int32)
    earlier = (order[None, :] < order[:, None])[None]
    same = flat[:, :, None] == flat[:, None, :]
    place = jnp.sum(jnp.where(jnp.logical_and(same, earlier), 1, 0), axis=2)
    seat = jnp.where(place < cap, flat * cap + place, -1)
    seat = seat.reshape(micro, toks, top).transpose(0, 2, 1)
    ids = ids.transpose(0, 2, 1)
    if extra:
        quarter = jnp.arange(fold, dtype=jnp.int32)[None, :, None] * extra
        side = (flat * cap + place - cap)[:, None, :] + quarter
        side = jnp.where((place >= cap)[:, None, :], side, -1)
        side = side.reshape(micro, fold, toks, top).transpose(0, 3, 1, 2)
        side = side.reshape(micro, top, fold * toks)
    else:
        side = seat
    vmem = pl.BlockSpec(memory_space=pltpu.VMEM)
    hbm = pl.BlockSpec(memory_space=pl.ANY)
    out_rows, grad_rows = pl.pallas_call(
        functools.partial(kernel, sections, experts, cap, extra),
        out_shape=(jax.ShapeDtypeStruct(x0.shape, BF16), jax.ShapeDtypeStruct(x0.shape, BF16)),
        in_specs=[vmem] * 9 + [hbm] * 3,
        out_specs=(vmem, vmem),
        scratch_shapes=[
            pltpu.VMEM((feat, hidden), BF16),
            pltpu.VMEM((feat, hidden), BF16),
            pltpu.VMEM((hidden, feat), BF16),
            pltpu.VMEM((micro, toks, feat), BF16),
            pltpu.VMEM((micro, toks, feat), BF16),
            pltpu.VMEM((2, micro, places, count * room), BF16),
            pltpu.VMEM((2 * micro, places, count * room), BF16),
            pltpu.VMEM((4 * micro, places, relayed * room), BF16),
            pltpu.VMEM((micro, places, 128), F32),
            pltpu.VMEM((micro, places, 128), F32),
            pltpu.VMEM((micro, every, hidden), F32),
            pltpu.VMEM((micro, every, hidden), F32),
            pltpu.VMEM((every, hidden), F32),
            pltpu.VMEM((every, hidden), BF16),
            pltpu.VMEM((every, hidden), BF16),
            pltpu.VMEM((every, PIECE), BF16),
            pltpu.VMEM((micro, top, toks, feat), BF16),
            pltpu.VMEM((micro, toks, feat), F32),
            pltpu.VMEM((micro, 2 + 3 * top, toks, 1), F32),
            pltpu.VMEM((1 + top, toks, 1), F32),
            pltpu.VMEM((toks, experts), F32),
            pltpu.VMEM((micro, top, places, toks), BF16),
            pltpu.VMEM((micro, top, toks, places), BF16),
            pltpu.VMEM((micro, top, places, side.shape[2]), BF16),
            pltpu.VMEM((micro, top, side.shape[2], places), BF16),
            pltpu.SemaphoreType.DMA((3,)),
            pltpu.SemaphoreType.DMA((2, micro, count)),
            pltpu.SemaphoreType.DMA((4 * micro, count)),
            pltpu.SemaphoreType.DMA((4 * micro, count)),
            pltpu.SemaphoreType.DMA((4 * micro, count)),
            pltpu.SemaphoreType.DMA((4 * micro, relayed, experts)),
            pltpu.SemaphoreType.DMA((4 * micro, count)),
            pltpu.SemaphoreType.DMA((4 * micro, count)),
            pltpu.SemaphoreType.DMA((2, micro, count)),
            pltpu.SemaphoreType.DMA((2, micro, count)),
            pltpu.SemaphoreType.DMA((micro,)),
            pltpu.SemaphoreType.DMA((micro,)),
            pltpu.SemaphoreType.DMA((micro,)),
        ],
        compiler_params=pltpu.CompilerParams(
            collective_id=0, has_side_effects=True, vmem_limit_bytes=62 * 1024 * 1024
        ),
    )(
        x0,
        cotangent,
        norm_gain,
        router[0].T,
        seat[:, :, None, :],
        seat[:, :, :, None],
        side[:, :, None, :],
        side[:, :, :, None],
        ids[:, :, :, None],
        w_gate[0, 0],
        w_up[0, 0],
        w_down[0, 0],
    )
    return (out_rows[None], grad_rows[None])


def solution(mesh):
    placed = (
        P(None, "expert", None),
        P(None, "expert", None),
        P("pipe", None, "expert", None),
        P("pipe", None),
        P("pipe", None, None),
        P("pipe", "expert", None, None),
        P("pipe", "expert", None, None),
        P("pipe", "expert", None, None),
    )
    return jax.shard_map(
        local,
        mesh=mesh,
        in_specs=placed,
        out_specs=(P("pipe", None, "expert", None), P("pipe", None, "expert", None)),
        check_vma=False,
    )
```

```python
import functools

import jax
import jax.numpy as jnp
from jax import lax
from jax.experimental import pallas as pl
from jax.experimental.pallas import tpu as pltpu
from jax.sharding import PartitionSpec as P

EPS = 1e-06
ROUTE_SCALE = 2.5
MESH = pl.DeviceIdType.MESH
F32 = jnp.float32
BF16 = jnp.bfloat16
PIECE = 512
LEAD = 2
HIGHEST = lax.Precision.HIGHEST
NEAR, FAR, BOTH = range(3)


def dot_nn(a, b):
    return jnp.dot(a, b, preferred_element_type=F32)


def dot_nt(a, b, precision=None):
    return lax.dot_general(
        a, b, (((1,), (1,)), ((), ())), preferred_element_type=F32, precision=precision
    )


def roles_of(count, all_both):
    if all_both:
        middle = count // 2
        return (BOTH,) * middle + (NEAR,) + (BOTH,) * (count - 1 - middle)
    return tuple(FAR if i % 2 else NEAR for i in range(count))


def split_of(capacity):
    extra = capacity - 16
    if extra in (1, 2, 4, 8):
        return 16, extra
    return -(-capacity // 8) * 8, 0


def stack(rows, parts):
    width = rows.shape[1] // parts
    return jnp.concatenate([rows[:, q * width : (q + 1) * width] for q in range(parts)], axis=0)


def unstack(rows, parts):
    height = rows.shape[0] // parts
    return jnp.concatenate([rows[q * height : (q + 1) * height] for q in range(parts)], axis=1)


def one_hot(rows_at, cols_at):
    return jnp.where(rows_at == cols_at, 1.0, 0.0).astype(BF16)


def kernel(
    sections,
    experts,
    cap,
    extra,
    x0_ref,
    cot_ref,
    gain_ref,
    router_ref,
    seat_row,
    seat_col,
    fold_row,
    fold_col,
    id_col,
    wg_hbm,
    wu_hbm,
    wd_hbm,
    out_ref,
    grad_ref,
    wg,
    wu,
    wd,
    xin,
    gin,
    send,
    recv,
    relay,
    row_send,
    row_recv,
    gproj,
    uproj,
    dhid,
    act_a,
    act_b,
    lhs,
    slots,
    base,
    stats,
    sums,
    scores,
    squares,
    tab,
    tabt,
    ftab,
    ftabt,
    folds,
    wsem,
    lsem,
    ssem,
    rsem,
    vssem,
    vrsem,
    fssem,
    frsem,
    pssem,
    prsem,
    tssem,
    trsem,
    tlsem,
):
    sec = lax.axis_index("pipe")
    me = lax.axis_index("expert")
    micro, toks, feat = x0_ref.shape
    hidden = wg.shape[1]
    top = seat_row.shape[1]
    places = experts * cap
    fold = 16 // extra if extra else 0
    count = feat // PIECE
    room = send.shape[3] // count
    ways = (roles_of(count, extra > 0),) * 2
    relayed = [[c for c in range(count) if way[c] != NEAR] for way in ways]
    half = feat // 2
    helper = lax.rem(sec + sections // 2, sections)
    hc = 512 if hidden % 512 == 0 else hidden
    inv_feat = 1.0 / feat
    parity = lax.rem(me, 2)
    others = pl.ds(0, (experts - 1) * cap)

    loads = [
        pltpu.make_async_copy(src, dst, wsem.at[i])
        for i, (src, dst) in enumerate(((wg_hbm, wg), (wu_hbm, wu), (wd_hbm, wd)))
    ]
    for load in loads:
        load.start()

    barrier = pltpu.get_barrier_semaphore()

    def greet(i, carry):
        pl.semaphore_signal(
            barrier, inc=1, device_id=(sec, lax.rem(me + i, experts)), device_id_type=MESH
        )
        return carry

    lax.fori_loop(1, experts, greet, 0)

    def greet_helper(i, carry):
        pl.semaphore_signal(barrier, inc=1, device_id=(helper, i), device_id_type=MESH)
        return carry

    lax.fori_loop(0, experts, greet_helper, 0)

    @pl.when(sec > 0)
    def _():
        pl.semaphore_signal(barrier, inc=1, device_id=(sec - 1, me), device_id_type=MESH)

    @pl.when(sec < sections - 1)
    def _():
        pl.semaphore_signal(barrier, inc=1, device_id=(sec + 1, me), device_id_type=MESH)

    neighbours = jnp.where(sec > 0, 1, 0) + jnp.where(sec < sections - 1, 1, 0)
    pl.semaphore_wait(barrier, 2 * experts - 1 + neighbours)

    def rows_of(e):
        return pl.ds(pl.multiple_of(e * cap, cap), cap)

    def cols(c, width):
        return pl.ds(pl.multiple_of(c * width, width), width)

    def piece(c):
        return pl.ds(c * PIECE, PIECE)

    def packed(c):
        return pl.ds(c * room, room)

    def relay_cols(p, c):
        return pl.ds(relayed[p % 2].index(c) * room, room)

    chips = experts // 2
    side_chips = chips // 2
    across = experts // 4

    def each_other(body):
        body(2 * (me // 2) + 1 - parity, True, False)
        here = (me // 2) // side_chips
        spot = lax.rem(me // 2, side_chips)

        def chip(i, beyond):
            there = (1 - here if beyond else here) * side_chips
            there = 2 * (there + lax.rem(spot + i, side_chips))
            body(there + parity, False, False)
            body(there + 1 - parity, False, beyond)

        for beyond in (True, False):
            first = 0 if beyond else 1
            if chips <= 4:
                for i in range(first, side_chips):
                    chip(i, beyond)
            else:
                lax.fori_loop(first, side_chips, lambda i, carry: chip(i, beyond), None)

    def slot_of(p, m):
        return p * micro + m

    def land_of(p, m):
        return (p % 2) * micro + m

    def direct(p, m, c, near, rows_src, rows_dst, peer):
        return pltpu.make_async_remote_copy(
            src_ref=send.at[p % 2, m, rows_src, packed(c)],
            dst_ref=recv.at[land_of(p, m), rows_dst, packed(c)],
            send_sem=(ssem if near else vssem).at[slot_of(p, m), c],
            recv_sem=(rsem if near else frsem).at[slot_of(p, m), c],
            device_id=(sec, peer),
            device_id_type=MESH,
        )

    def to_helper(p, m, c, peer):
        return pltpu.make_async_remote_copy(
            src_ref=send.at[p % 2, m, rows_of(peer), packed(c)],
            dst_ref=relay.at[slot_of(p, m), rows_of(peer), relay_cols(p, c)],
            send_sem=vssem.at[slot_of(p, m), c],
            recv_sem=vrsem.at[slot_of(p, m), relayed[p % 2].index(c), peer],
            device_id=(helper, me),
            device_id_type=MESH,
        )

    def from_helper(p, m, c, rows_src, rows_dst, mark):
        return pltpu.make_async_remote_copy(
            src_ref=relay.at[slot_of(p, m), rows_src, relay_cols(p, c)],
            dst_ref=recv.at[land_of(p, m), rows_dst, packed(c)],
            send_sem=fssem.at[slot_of(p, m), c],
            recv_sem=frsem.at[slot_of(p, m), c],
            device_id=(helper, mark),
            device_id_type=MESH,
        )

    def own_copy(p, m, c):
        return pltpu.make_async_copy(
            send.at[p % 2, m, rows_of(me), packed(c)],
            recv.at[land_of(p, m), rows_of(me), packed(c)],
            lsem.at[p % 2, m, c],
        )

    def start(p, m, c):
        way = ways[p % 2][c]

        def one(peer, mate, beyond):
            near = way == NEAR or (way == BOTH and not beyond)
            if near or mate:
                direct(p, m, c, near, rows_of(peer), rows_of(me), peer).start()
            else:
                to_helper(p, m, c, peer).start()

        each_other(one)
        own_copy(p, m, c).start()

    def arrive(p, m, c):
        own_copy(p, m, c).wait()
        other = lax.rem(me + 1, experts)
        for near, alone in ((True, NEAR), (False, FAR)):
            way = ways[p % 2][c]
            if way == BOTH:
                some = pl.ds(0, (experts - 1 - across if near else across) * cap)
                direct(p, m, c, near, some, some, other).wait()
            elif way == alone:
                direct(p, m, c, near, others, others, other).wait()

    def relay_pass(p, m):
        for c in relayed[p % 2]:
            both = ways[p % 2][c] == BOTH

            def one(mark, mate, beyond):
                if not mate and (beyond or not both):
                    to_helper(p, m, c, mark).wait_recv()
                    from_helper(p, m, c, rows_of(mark), rows_of(me), mark).start()

            each_other(one)
        for c in relayed[p % 2]:
            both = ways[p % 2][c] == BOTH
            some = pl.ds(0, (across if both else experts - 2) * cap)
            from_helper(p, m, c, some, some, lax.rem(me + 2, experts)).wait_send()

    def hop(src, dst, d, m, c, to):
        return pltpu.make_async_remote_copy(
            src_ref=src.at[m, :, piece(c)],
            dst_ref=dst.at[m, :, piece(c)],
            send_sem=pssem.at[d, m, c],
            recv_sem=prsem.at[d, m, c],
            device_id=(to, me),
            device_id_type=MESH,
        )

    def pair_of(ref, m):
        return ref[m, top]

    def make_tables():
        def at(shape, dim):
            return lax.broadcasted_iota(jnp.int32, shape, dim)

        for m in range(micro):
            for k in range(top):
                tab[m, k] = one_hot(at((places, toks), 0), seat_row[m, k])
                tabt[m, k] = one_hot(at((toks, places), 1), seat_col[m, k])
                if extra:
                    ftab[m, k] = one_hot(at((places, fold * toks), 0), fold_row[m, k])
                    ftabt[m, k] = one_hot(at((fold * toks, places), 1), fold_col[m, k])
            for table in (tab, tabt) + ((ftab, ftabt) if extra else ()):
                table[m, top] = functools.reduce(jnp.add, [table[m, k] for k in range(top)])
        if extra:
            for dim in (0, 1):
                folds[dim] = folding(dim)

    def folding(dim):
        low = extra.bit_length() - 1
        rows = (experts * extra).bit_length() - 1
        long = lax.broadcasted_iota(jnp.int32, (places, places), dim)
        short = lax.broadcasted_iota(jnp.int32, (places, places), 1 - dim)
        group = jnp.right_shift(long, rows)
        within = jnp.bitwise_and(long, (1 << rows) - 1)
        block = jnp.right_shift(within, low)
        return one_hot(block * cap + group * extra + jnp.bitwise_and(within, extra - 1), short)

    def unfolded(p, m, c):
        land = land_of(p, m)
        main = recv[land, :, pl.ds(c * room, PIECE)]
        if not extra:
            return main
        folded = recv[land, :, pl.ds(c * room + PIECE, room - PIECE)]
        more = unstack(dot_nn(folds[0], folded).astype(BF16), fold)
        return jnp.concatenate([main, more], axis=0)

    def put_results(m, c, result):
        send[1, m, :, pl.ds(c * room, PIECE)] = result[:places]
        if extra:
            send[1, m, :, pl.ds(c * room + PIECE, room - PIECE)] = dot_nn(
                folds[1], stack(result[places:], fold)
            ).astype(BF16)

    def put_rows(m, c, pairs):
        placed = functools.reduce(jnp.add, [dot_nn(main, rows) for main, _, rows in pairs])
        send[0, m, :, pl.ds(c * room, PIECE)] = placed.astype(BF16)
        if extra:
            placed = functools.reduce(
                jnp.add, [dot_nn(side, stack(rows, fold)) for _, side, rows in pairs]
            )
            send[0, m, :, pl.ds(c * room + PIECE, room - PIECE)] = placed.astype(BF16)

    def taken(p, m, c, main, side):
        land = land_of(p, m)
        rows = dot_nn(main, recv[land, :, pl.ds(c * room, PIECE)])
        if extra:
            folded = recv[land, :, pl.ds(c * room + PIECE, room - PIECE)]
            rows = rows + unstack(dot_nn(side, folded), fold)
        return rows

    def take(ref, whole, land, d, m, c, first, before):
        @pl.when(first)
        def _():
            land[m, :, piece(c)] = whole[m, :, piece(c)]

        @pl.when(jnp.logical_not(first))
        def _():
            hop(ref, land, d, m, c, before).wait_recv()

    def pick(m, k):
        lanes = lax.broadcasted_iota(jnp.int32, (toks, experts), 1)
        return jnp.where(lanes == id_col[m, k], 1.0, 0.0)

    def gates_of(m):
        inv_rms = lax.rsqrt(sums[0] * inv_feat + EPS)
        logits = scores[...] * inv_rms
        chosen = [jnp.sum(pick(m, k) * logits, axis=-1, keepdims=True) for k in range(top)]
        affinity = [jax.nn.sigmoid(c) for c in chosen]
        aff_total = functools.reduce(jnp.add, affinity)
        stats[m, 0] = inv_rms
        for k in range(top):
            stats[m, 2 + k] = affinity[k]
            stats[m, 2 + top + k] = ROUTE_SCALE * affinity[k] / aff_total
            stats[m, 2 + 2 * top + k] = chosen[k]

    def to_experts(m, c):
        at = piece(c)
        main = pair_of(tab, m)
        side = pair_of(ftab, m) if extra else None
        take(out_ref, x0_ref, xin, 0, m, c, sec == 0, sec - 1)
        put_rows(m, c, [(main, side, xin[m, :, at])])
        start(0, m, c)
        v = xin[m, :, at].astype(F32)
        own = jnp.sum(v * v, axis=-1, keepdims=True)
        logits = dot_nt((v * gain_ref[:, at]).astype(BF16), router_ref[:, at])
        sums[0] = own if c == 0 else sums[0] + own
        scores[...] = logits if c == 0 else scores[...] + logits

    def expert_up(m, c):
        at = piece(c)
        arrive(0, m, c)
        if c == 0 and m == 0:
            for load in loads:
                load.wait()
        v = unfolded(0, m, c).astype(F32)
        own = jnp.sum(v * v, axis=-1, keepdims=True)
        squares[...] = own if c == 0 else squares[...] + own
        lhs[...] = (v * gain_ref[:, at]).astype(BF16)
        g = dot_nn(lhs[...], wg[at, :])
        u = dot_nn(lhs[...], wu[at, :])
        gproj[m] = g if c == 0 else gproj[m] + g
        uproj[m] = u if c == 0 else uproj[m] + u

    def expert_act(m):
        inv_rms = lax.rsqrt(squares[...] * inv_feat + EPS)

        def activate(c, carry):
            hat = cols(c, hc)
            g = gproj[m, :, hat] * inv_rms
            u = uproj[m, :, hat] * inv_rms
            gproj[m, :, hat] = g
            uproj[m, :, hat] = u
            act_a[:, hat] = (g * jax.nn.sigmoid(g) * u).astype(BF16)
            return carry

        lax.fori_loop(0, hidden // hc, activate, 0)

    def expert_down(m):
        for c in range(count):
            put_results(m, c, dot_nn(act_a[...], wd[:, piece(c)]).astype(BF16))
            start(1, m, c)

    def combine(m, c):
        gates = [stats[m, 2 + top + k] for k in range(top)]
        at = piece(c)
        arrive(1, m, c)
        mixed = jnp.zeros((toks, PIECE), F32)
        for k in range(top):
            side = ftabt[m, k] if extra else None
            part = taken(1, m, c, tabt[m, k], side).astype(BF16)
            slots[m, k, :, at] = part
            mixed = mixed + gates[k] * part.astype(F32)
        out_ref[m, :, at] = (xin[m, :, at].astype(F32) + mixed).astype(BF16)

        @pl.when(sec < sections - 1)
        def _():
            hop(out_ref, xin, 0, m, c, sec + 1).start()

    def grads_to_experts(m, c):
        gates = [stats[m, 2 + top + k] for k in range(top)]
        at = piece(c)
        take(grad_ref, cot_ref, gin, 1, m, c, sec == sections - 1, sec + 1)
        dy = gin[m, :, at].astype(F32)
        put_rows(
            m,
            c,
            [
                (tab[m, k], ftab[m, k] if extra else None, (gates[k] * dy).astype(BF16))
                for k in range(top)
            ],
        )
        start(2, m, c)
        for k in range(top):
            own = jnp.sum(dy * slots[m, k, :, at].astype(F32), axis=-1, keepdims=True)
            sums[1 + k] = own if c == 0 else sums[1 + k] + own

    def expert_hidden_grad(m, c):
        arrive(2, m, c)
        lhs[...] = unfolded(2, m, c)
        d = dot_nt(lhs[...], wd[:, piece(c)])
        dhid[...] = d if c == 0 else dhid[...] + d

    def router_grad(m):
        inv_rms = stats[m, 0]
        affinity = [stats[m, 2 + k] for k in range(top)]
        gates = [stats[m, 2 + top + k] for k in range(top)]
        aff_total = functools.reduce(jnp.add, affinity)
        dgates = [sums[1 + k] for k in range(top)]
        inner = functools.reduce(jnp.add, [d * g for d, g in zip(dgates, gates)]) / ROUTE_SCALE
        dlog = jnp.zeros((toks, experts), F32)
        along = jnp.zeros((toks, 1), F32)
        for k in range(top):
            daff = ROUTE_SCALE / aff_total * (dgates[k] - inner)
            dlogit = daff * affinity[k] * (1.0 - affinity[k])
            dlog = dlog + pick(m, k) * dlogit
            along = along + dlogit * stats[m, 2 + 2 * top + k]
        stats[m, 1] = along

        def spread(c, carry):
            at = cols(c, half)
            term = jnp.dot(
                dlog,
                router_ref[:, at].astype(F32),
                preferred_element_type=F32,
                precision=HIGHEST,
            )
            base[m, :, at] = gin[m, :, at].astype(F32) + inv_rms * gain_ref[:, at] * term
            return carry

        lax.fori_loop(0, 2, spread, 0)

    def row_copy(m, rows_src, rows_dst, peer):
        return pltpu.make_async_remote_copy(
            src_ref=row_send.at[m, rows_src],
            dst_ref=row_recv.at[m, rows_dst],
            send_sem=tssem.at[m],
            recv_sem=trsem.at[m],
            device_id=(sec, peer),
            device_id_type=MESH,
        )

    def own_row(m):
        return pltpu.make_async_copy(
            row_send.at[m, rows_of(me)], row_recv.at[m, rows_of(me)], tlsem.at[m]
        )

    def hidden_done(m):
        def activate(c, along):
            hat = cols(c, hc)
            dh = dhid[:, hat]
            g = gproj[m, :, hat]
            u = uproj[m, :, hat]
            s = jax.nn.sigmoid(g)
            a = (dh * u * s * (1.0 + g * (1.0 - s))).astype(BF16)
            b = (dh * g * s).astype(BF16)
            act_a[:, hat] = a
            act_b[:, hat] = b
            return along + jnp.sum(a.astype(F32) * g + b.astype(F32) * u, axis=-1, keepdims=True)

        along = jnp.zeros((lhs.shape[0], 1), F32)
        along = lax.fori_loop(0, hidden // hc, activate, along)
        message = jnp.broadcast_to(along[:places], row_send.shape[1:])
        if extra:
            few = jnp.broadcast_to(along[places:], (experts * extra, row_send.shape[2]))
            rest = jnp.zeros((places - experts * extra, row_send.shape[2]), F32)
            folded = jnp.dot(
                folds[1].astype(F32),
                jnp.concatenate([few, rest], axis=0),
                preferred_element_type=F32,
                precision=HIGHEST,
            )
            lanes = lax.broadcasted_iota(jnp.int32, row_send.shape[1:], 1)
            message = jnp.where(lanes == 0, message, folded)
        row_send[m] = message
        each_other(lambda peer, mate, beyond: row_copy(m, rows_of(peer), rows_of(me), peer).start())
        own_row(m).start()

    def row_sum(table, m):
        return jnp.dot(
            table.astype(F32), row_recv[m], preferred_element_type=F32, precision=HIGHEST
        )

    def expert_rows_grad(m):
        for c in range(count):
            at = piece(c)
            summed = dot_nt(act_a[...], wg[at, :]) + dot_nt(act_b[...], wu[at, :])
            put_results(m, c, summed.astype(BF16))
            start(3, m, c)

    def gather(m, c):
        inv_rms = stats[m, 0]
        at = piece(c)
        main = pair_of(tabt, m)
        side = pair_of(ftabt, m) if extra else None
        if c == 0:
            own_row(m).wait()
            row_copy(m, others, others, lax.rem(me + 1, experts)).wait()
            along = row_sum(main, m)[:, 0:1] + stats[m, 1]
            if extra:
                along = along + row_sum(side[:toks], m)[:, 1:2]
            stats[m, 1] = inv_rms * inv_rms * inv_feat * along
        arrive(3, m, c)
        dn = taken(3, m, c, main, side)
        grad_ref[m, :, at] = (
            base[m, :, at]
            + inv_rms * (gain_ref[:, at] * dn)
            - xin[m, :, at].astype(F32) * stats[m, 1]
        ).astype(BF16)

        @pl.when(sec > 0)
        def _():
            hop(grad_ref, gin, 1, m, c, sec - 1).start()

    def weave(inward, m, outward, before):
        for c in range(count + LEAD):
            if c >= LEAD:
                outward(before, c - LEAD)
            if c < count:
                inward(m, c)

    def in_turn(body, m):
        for c in range(count):
            body(m, c)

    def relay_forward(m, carry):
        relay_pass(0, m)
        relay_pass(1, m)
        return carry

    def relay_backward(m, carry):
        relay_pass(2, m)
        relay_pass(3, m)
        return carry

    make_tables()
    early = sec < sections // 2

    @pl.when(jnp.logical_not(early))
    def _():
        lax.fori_loop(0, micro, relay_forward, 0)

    for m in range(micro):
        if m == 0:
            in_turn(to_experts, m)
            gates_of(m)
            in_turn(expert_up, m)
        else:
            weave(to_experts, m, combine, m - 1)
            in_turn(expert_up, m)
        expert_act(m)
        expert_down(m)
        if m > 0:
            gates_of(m)

    @pl.when(sec == sections - 1)
    def _():
        weave(grads_to_experts, 0, combine, micro - 1)

    @pl.when(sec < sections - 1)
    def _():
        in_turn(combine, micro - 1)

        @pl.when(early)
        def _():
            lax.fori_loop(0, micro, relay_forward, 0)
            lax.fori_loop(0, micro, relay_backward, 0)

        in_turn(grads_to_experts, 0)

    for m in range(micro):
        if m == 0:
            router_grad(m)
            in_turn(expert_hidden_grad, m)
        else:
            weave(grads_to_experts, m, gather, m - 1)
            in_turn(expert_hidden_grad, m)
        hidden_done(m)
        expert_rows_grad(m)
        if m > 0:
            router_grad(m)
    in_turn(gather, micro - 1)

    @pl.when(jnp.logical_not(early))
    def _():
        lax.fori_loop(0, micro, relay_backward, 0)

    def drain(m, carry):
        @pl.when(sec < sections - 1)
        def _():
            for c in range(count):
                hop(out_ref, xin, 0, m, c, sec + 1).wait_send()

        @pl.when(sec > 0)
        def _():
            for c in range(count):
                hop(grad_ref, gin, 1, m, c, sec - 1).wait_send()

        return carry

    lax.fori_loop(0, micro, drain, 0)


def local(x0, cotangent, expert_ids, norm_gain, router, w_gate, w_up, w_down):
    sections = lax.axis_size("pipe")
    experts = lax.axis_size("expert")
    micro, toks, feat = x0.shape
    top = expert_ids.shape[3]
    cap, extra = split_of(toks * top * 5 // (4 * experts))
    fold = 16 // extra if extra else 0
    places = experts * cap
    every = places + experts * extra
    count = feat // PIECE
    room = PIECE + (PIECE // fold if extra else 0)
    relayed = sum(way != NEAR for way in roles_of(count, extra > 0))
    hidden = w_gate.shape[3]
    ids = expert_ids[0]
    flat = ids.reshape(micro, toks * top)
    order = jnp.arange(toks * top, dtype=jnp.int32)
    earlier = (order[None, :] < order[:, None])[None]
    same = flat[:, :, None] == flat[:, None, :]
    place = jnp.sum(jnp.where(jnp.logical_and(same, earlier), 1, 0), axis=2)
    seat = jnp.where(place < cap, flat * cap + place, -1)
    seat = seat.reshape(micro, toks, top).transpose(0, 2, 1)
    ids = ids.transpose(0, 2, 1)
    if extra:
        quarter = jnp.arange(fold, dtype=jnp.int32)[None, :, None] * extra
        side = (flat * cap + place - cap)[:, None, :] + quarter
        side = jnp.where((place >= cap)[:, None, :], side, -1)
        side = side.reshape(micro, fold, toks, top).transpose(0, 3, 1, 2)
        side = side.reshape(micro, top, fold * toks)
    else:
        side = seat
    vmem = pl.BlockSpec(memory_space=pltpu.VMEM)
    hbm = pl.BlockSpec(memory_space=pl.ANY)
    out_rows, grad_rows = pl.pallas_call(
        functools.partial(kernel, sections, experts, cap, extra),
        out_shape=(jax.ShapeDtypeStruct(x0.shape, BF16), jax.ShapeDtypeStruct(x0.shape, BF16)),
        in_specs=[vmem] * 9 + [hbm] * 3,
        out_specs=(vmem, vmem),
        scratch_shapes=[
            pltpu.VMEM((feat, hidden), BF16),
            pltpu.VMEM((feat, hidden), BF16),
            pltpu.VMEM((hidden, feat), BF16),
            pltpu.VMEM((micro, toks, feat), BF16),
            pltpu.VMEM((micro, toks, feat), BF16),
            pltpu.VMEM((2, micro, places, count * room), BF16),
            pltpu.VMEM((2 * micro, places, count * room), BF16),
            pltpu.VMEM((4 * micro, places, relayed * room), BF16),
            pltpu.VMEM((micro, places, 128), F32),
            pltpu.VMEM((micro, places, 128), F32),
            pltpu.VMEM((micro, every, hidden), F32),
            pltpu.VMEM((micro, every, hidden), F32),
            pltpu.VMEM((every, hidden), F32),
            pltpu.VMEM((every, hidden), BF16),
            pltpu.VMEM((every, hidden), BF16),
            pltpu.VMEM((every, PIECE), BF16),
            pltpu.VMEM((micro, top, toks, feat), BF16),
            pltpu.VMEM((micro, toks, feat), F32),
            pltpu.VMEM((micro, 2 + 3 * top, toks, 1), F32),
            pltpu.VMEM((1 + top, toks, 1), F32),
            pltpu.VMEM((toks, experts), F32),
            pltpu.VMEM((every, 1), F32),
            pltpu.VMEM((micro, top + 1, places, toks), BF16),
            pltpu.VMEM((micro, top + 1, toks, places), BF16),
            pltpu.VMEM((micro, top + 1, places, side.shape[2]), BF16),
            pltpu.VMEM((micro, top + 1, side.shape[2], places), BF16),
            pltpu.VMEM((2, places, places) if extra else (2, 16, 128), BF16),
            pltpu.SemaphoreType.DMA((3,)),
            pltpu.SemaphoreType.DMA((2, micro, count)),
            pltpu.SemaphoreType.DMA((4 * micro, count)),
            pltpu.SemaphoreType.DMA((4 * micro, count)),
            pltpu.SemaphoreType.DMA((4 * micro, count)),
            pltpu.SemaphoreType.DMA((4 * micro, relayed, experts)),
            pltpu.SemaphoreType.DMA((4 * micro, count)),
            pltpu.SemaphoreType.DMA((4 * micro, count)),
            pltpu.SemaphoreType.DMA((2, micro, count)),
            pltpu.SemaphoreType.DMA((2, micro, count)),
            pltpu.SemaphoreType.DMA((micro,)),
            pltpu.SemaphoreType.DMA((micro,)),
            pltpu.SemaphoreType.DMA((micro,)),
        ],
        compiler_params=pltpu.CompilerParams(
            collective_id=0, has_side_effects=True, vmem_limit_bytes=62 * 1024 * 1024
        ),
    )(
        x0,
        cotangent,
        norm_gain,
        router[0].T,
        seat[:, :, None, :],
        seat[:, :, :, None],
        side[:, :, None, :],
        side[:, :, :, None],
        ids[:, :, :, None],
        w_gate[0, 0],
        w_up[0, 0],
        w_down[0, 0],
    )
    return (out_rows[None], grad_rows[None])


def solution(mesh):
    placed = (
        P(None, "expert", None),
        P(None, "expert", None),
        P("pipe", None, "expert", None),
        P("pipe", None),
        P("pipe", None, None),
        P("pipe", "expert", None, None),
        P("pipe", "expert", None, None),
        P("pipe", "expert", None, None),
    )
    return jax.shard_map(
        local,
        mesh=mesh,
        in_specs=placed,
        out_specs=(P("pipe", None, "expert", None), P("pipe", None, "expert", None)),
        check_vma=False,
    )
```

```python
import functools

import jax
import jax.numpy as jnp
from jax import lax
from jax.experimental import pallas as pl
from jax.experimental.pallas import tpu as pltpu
from jax.sharding import PartitionSpec as P

EPS = 1e-06
ROUTE_SCALE = 2.5
MESH = pl.DeviceIdType.MESH
F32 = jnp.float32
BF16 = jnp.bfloat16
PIECE = 512
LEAD = 1
HIGHEST = lax.Precision.HIGHEST
NEAR, FAR, BOTH = range(3)


def dot_nn(a, b):
    return jnp.dot(a, b, preferred_element_type=F32)


def dot_nt(a, b, precision=None):
    return lax.dot_general(
        a, b, (((1,), (1,)), ((), ())), preferred_element_type=F32, precision=precision
    )


def roles_of(count, all_both):
    if all_both:
        middle = count // 2
        return (BOTH,) * middle + (NEAR,) + (BOTH,) * (count - 1 - middle)
    return tuple(FAR if i % 2 else NEAR for i in range(count))


def split_of(capacity):
    extra = capacity - 16
    if extra in (1, 2, 4, 8):
        return 16, extra
    return -(-capacity // 8) * 8, 0


def stack(rows, parts):
    width = rows.shape[1] // parts
    return jnp.concatenate([rows[:, q * width : (q + 1) * width] for q in range(parts)], axis=0)


def unstack(rows, parts):
    height = rows.shape[0] // parts
    return jnp.concatenate([rows[q * height : (q + 1) * height] for q in range(parts)], axis=1)


def one_hot(rows_at, cols_at):
    return jnp.where(rows_at == cols_at, 1.0, 0.0).astype(BF16)


def kernel(
    sections,
    experts,
    cap,
    extra,
    x0_ref,
    cot_ref,
    gain_ref,
    router_ref,
    seat_row,
    seat_col,
    fold_row,
    fold_col,
    id_col,
    wg_hbm,
    wu_hbm,
    wd_hbm,
    out_ref,
    grad_ref,
    wg,
    wu,
    wd,
    xin,
    gin,
    send,
    recv,
    relay,
    row_send,
    row_recv,
    gproj,
    uproj,
    dhid,
    act_a,
    act_b,
    lhs,
    slots,
    base,
    stats,
    sums,
    scores,
    squares,
    tab,
    tabt,
    ftab,
    ftabt,
    folds,
    wsem,
    lsem,
    ssem,
    rsem,
    vssem,
    vrsem,
    fssem,
    frsem,
    pssem,
    prsem,
    tssem,
    trsem,
    tlsem,
):
    sec = lax.axis_index("pipe")
    me = lax.axis_index("expert")
    micro, toks, feat = x0_ref.shape
    hidden = wg.shape[1]
    top = seat_row.shape[1]
    places = experts * cap
    fold = 16 // extra if extra else 0
    count = feat // PIECE
    room = send.shape[3] // count
    ways = (roles_of(count, extra > 0),) * 2
    relayed = [[c for c in range(count) if way[c] != NEAR] for way in ways]
    half = feat // 2
    helper = lax.rem(sec + sections // 2, sections)
    hc = 512 if hidden % 512 == 0 else hidden
    inv_feat = 1.0 / feat
    parity = lax.rem(me, 2)
    others = pl.ds(0, (experts - 1) * cap)

    loads = [
        pltpu.make_async_copy(src, dst, wsem.at[i])
        for i, (src, dst) in enumerate(((wg_hbm, wg), (wu_hbm, wu), (wd_hbm, wd)))
    ]
    for load in loads:
        load.start()

    barrier = pltpu.get_barrier_semaphore()

    def greet(i, carry):
        pl.semaphore_signal(
            barrier, inc=1, device_id=(sec, lax.rem(me + i, experts)), device_id_type=MESH
        )
        return carry

    lax.fori_loop(1, experts, greet, 0)

    def greet_helper(i, carry):
        pl.semaphore_signal(barrier, inc=1, device_id=(helper, i), device_id_type=MESH)
        return carry

    lax.fori_loop(0, experts, greet_helper, 0)

    @pl.when(sec > 0)
    def _():
        pl.semaphore_signal(barrier, inc=1, device_id=(sec - 1, me), device_id_type=MESH)

    @pl.when(sec < sections - 1)
    def _():
        pl.semaphore_signal(barrier, inc=1, device_id=(sec + 1, me), device_id_type=MESH)

    neighbours = jnp.where(sec > 0, 1, 0) + jnp.where(sec < sections - 1, 1, 0)
    pl.semaphore_wait(barrier, 2 * experts - 1 + neighbours)

    def rows_of(e):
        return pl.ds(pl.multiple_of(e * cap, cap), cap)

    def cols(c, width):
        return pl.ds(pl.multiple_of(c * width, width), width)

    def piece(c):
        return pl.ds(c * PIECE, PIECE)

    def packed(c):
        return pl.ds(c * room, room)

    def relay_cols(p, c):
        return pl.ds(relayed[p % 2].index(c) * room, room)

    chips = experts // 2
    side_chips = chips // 2
    across = experts // 4

    def each_other(body):
        body(2 * (me // 2) + 1 - parity, True, False)
        here = (me // 2) // side_chips
        spot = lax.rem(me // 2, side_chips)

        def chip(i, beyond):
            there = (1 - here if beyond else here) * side_chips
            there = 2 * (there + lax.rem(spot + i, side_chips))
            body(there + parity, False, False)
            body(there + 1 - parity, False, beyond)

        for beyond in (True, False):
            first = 0 if beyond else 1
            if chips <= 4:
                for i in range(first, side_chips):
                    chip(i, beyond)
            else:
                lax.fori_loop(first, side_chips, lambda i, carry: chip(i, beyond), None)

    def slot_of(p, m):
        return p * micro + m

    def land_of(p, m):
        return (p % 2) * micro + m

    def direct(p, m, c, near, rows_src, rows_dst, peer):
        return pltpu.make_async_remote_copy(
            src_ref=send.at[p % 2, m, rows_src, packed(c)],
            dst_ref=recv.at[land_of(p, m), rows_dst, packed(c)],
            send_sem=(ssem if near else vssem).at[slot_of(p, m), c],
            recv_sem=(rsem if near else frsem).at[slot_of(p, m), c],
            device_id=(sec, peer),
            device_id_type=MESH,
        )

    def to_helper(p, m, c, peer):
        return pltpu.make_async_remote_copy(
            src_ref=send.at[p % 2, m, rows_of(peer), packed(c)],
            dst_ref=relay.at[slot_of(p, m), rows_of(peer), relay_cols(p, c)],
            send_sem=vssem.at[slot_of(p, m), c],
            recv_sem=vrsem.at[slot_of(p, m), relayed[p % 2].index(c), peer],
            device_id=(helper, me),
            device_id_type=MESH,
        )

    def from_helper(p, m, c, rows_src, rows_dst, mark):
        return pltpu.make_async_remote_copy(
            src_ref=relay.at[slot_of(p, m), rows_src, relay_cols(p, c)],
            dst_ref=recv.at[land_of(p, m), rows_dst, packed(c)],
            send_sem=fssem.at[slot_of(p, m), c],
            recv_sem=frsem.at[slot_of(p, m), c],
            device_id=(helper, mark),
            device_id_type=MESH,
        )

    def own_copy(p, m, c):
        return pltpu.make_async_copy(
            send.at[p % 2, m, rows_of(me), packed(c)],
            recv.at[land_of(p, m), rows_of(me), packed(c)],
            lsem.at[p % 2, m, c],
        )

    def start(p, m, c):
        way = ways[p % 2][c]

        def one(peer, mate, beyond):
            near = way == NEAR or (way == BOTH and not beyond)
            if near or mate:
                direct(p, m, c, near, rows_of(peer), rows_of(me), peer).start()
            else:
                to_helper(p, m, c, peer).start()

        each_other(one)
        own_copy(p, m, c).start()

    def arrive(p, m, c):
        own_copy(p, m, c).wait()
        other = lax.rem(me + 1, experts)
        for near, alone in ((True, NEAR), (False, FAR)):
            way = ways[p % 2][c]
            if way == BOTH:
                some = pl.ds(0, (experts - 1 - across if near else across) * cap)
                direct(p, m, c, near, some, some, other).wait()
            elif way == alone:
                direct(p, m, c, near, others, others, other).wait()

    def relay_pass(p, m):
        for c in relayed[p % 2]:
            both = ways[p % 2][c] == BOTH

            def one(mark, mate, beyond):
                if not mate and (beyond or not both):
                    to_helper(p, m, c, mark).wait_recv()
                    from_helper(p, m, c, rows_of(mark), rows_of(me), mark).start()

            each_other(one)
        for c in relayed[p % 2]:
            both = ways[p % 2][c] == BOTH
            some = pl.ds(0, (across if both else experts - 2) * cap)
            from_helper(p, m, c, some, some, lax.rem(me + 2, experts)).wait_send()

    def hop(src, dst, d, m, c, to):
        return pltpu.make_async_remote_copy(
            src_ref=src.at[m, :, piece(c)],
            dst_ref=dst.at[m, :, piece(c)],
            send_sem=pssem.at[d, m, c],
            recv_sem=prsem.at[d, m, c],
            device_id=(to, me),
            device_id_type=MESH,
        )

    def pair_of(ref, m):
        return ref[m, top]

    def make_tables():
        def at(shape, dim):
            return lax.broadcasted_iota(jnp.int32, shape, dim)

        for m in range(micro):
            for k in range(top):
                tab[m, k] = one_hot(at((places, toks), 0), seat_row[m, k])
                tabt[m, k] = one_hot(at((toks, places), 1), seat_col[m, k])
                if extra:
                    ftab[m, k] = one_hot(at((places, fold * toks), 0), fold_row[m, k])
                    ftabt[m, k] = one_hot(at((fold * toks, places), 1), fold_col[m, k])
            for table in (tab, tabt) + ((ftab, ftabt) if extra else ()):
                table[m, top] = functools.reduce(jnp.add, [table[m, k] for k in range(top)])
        if extra:
            for dim in (0, 1):
                folds[dim] = folding(dim)

    def folding(dim):
        low = extra.bit_length() - 1
        rows = (experts * extra).bit_length() - 1
        long = lax.broadcasted_iota(jnp.int32, (places, places), dim)
        short = lax.broadcasted_iota(jnp.int32, (places, places), 1 - dim)
        group = jnp.right_shift(long, rows)
        within = jnp.bitwise_and(long, (1 << rows) - 1)
        block = jnp.right_shift(within, low)
        return one_hot(block * cap + group * extra + jnp.bitwise_and(within, extra - 1), short)

    def unfolded(p, m, c):
        land = land_of(p, m)
        main = recv[land, :, pl.ds(c * room, PIECE)]
        if not extra:
            return main
        folded = recv[land, :, pl.ds(c * room + PIECE, room - PIECE)]
        more = unstack(dot_nn(folds[0], folded).astype(BF16), fold)
        return jnp.concatenate([main, more], axis=0)

    def put_results(m, c, result):
        send[1, m, :, pl.ds(c * room, PIECE)] = result[:places]
        if extra:
            send[1, m, :, pl.ds(c * room + PIECE, room - PIECE)] = dot_nn(
                folds[1], stack(result[places:], fold)
            ).astype(BF16)

    def put_rows(m, c, pairs):
        placed = functools.reduce(jnp.add, [dot_nn(main, rows) for main, _, rows in pairs])
        send[0, m, :, pl.ds(c * room, PIECE)] = placed.astype(BF16)
        if extra:
            placed = functools.reduce(
                jnp.add, [dot_nn(side, stack(rows, fold)) for _, side, rows in pairs]
            )
            send[0, m, :, pl.ds(c * room + PIECE, room - PIECE)] = placed.astype(BF16)

    def taken(p, m, c, main, side):
        land = land_of(p, m)
        rows = dot_nn(main, recv[land, :, pl.ds(c * room, PIECE)])
        if extra:
            folded = recv[land, :, pl.ds(c * room + PIECE, room - PIECE)]
            rows = rows + unstack(dot_nn(side, folded), fold)
        return rows

    def take(ref, whole, land, d, m, c, first, before):
        @pl.when(first)
        def _():
            land[m, :, piece(c)] = whole[m, :, piece(c)]

        @pl.when(jnp.logical_not(first))
        def _():
            hop(ref, land, d, m, c, before).wait_recv()

    def pick(m, k):
        lanes = lax.broadcasted_iota(jnp.int32, (toks, experts), 1)
        return jnp.where(lanes == id_col[m, k], 1.0, 0.0)

    def gates_of(m):
        inv_rms = lax.rsqrt(sums[0] * inv_feat + EPS)
        logits = scores[...] * inv_rms
        chosen = [jnp.sum(pick(m, k) * logits, axis=-1, keepdims=True) for k in range(top)]
        affinity = [jax.nn.sigmoid(c) for c in chosen]
        aff_total = functools.reduce(jnp.add, affinity)
        stats[m, 0] = inv_rms
        for k in range(top):
            stats[m, 2 + k] = affinity[k]
            stats[m, 2 + top + k] = ROUTE_SCALE * affinity[k] / aff_total
            stats[m, 2 + 2 * top + k] = chosen[k]

    def to_experts(m, c):
        at = piece(c)
        main = pair_of(tab, m)
        side = pair_of(ftab, m) if extra else None
        take(out_ref, x0_ref, xin, 0, m, c, sec == 0, sec - 1)
        put_rows(m, c, [(main, side, xin[m, :, at])])
        start(0, m, c)
        v = xin[m, :, at].astype(F32)
        own = jnp.sum(v * v, axis=-1, keepdims=True)
        logits = dot_nt((v * gain_ref[:, at]).astype(BF16), router_ref[:, at])
        sums[0] = own if c == 0 else sums[0] + own
        scores[...] = logits if c == 0 else scores[...] + logits

    def expert_up(m, c):
        at = piece(c)
        arrive(0, m, c)
        if c == 0 and m == 0:
            for load in loads:
                load.wait()
        v = unfolded(0, m, c).astype(F32)
        own = jnp.sum(v * v, axis=-1, keepdims=True)
        squares[...] = own if c == 0 else squares[...] + own
        lhs[...] = (v * gain_ref[:, at]).astype(BF16)
        g = dot_nn(lhs[...], wg[at, :])
        u = dot_nn(lhs[...], wu[at, :])
        gproj[m] = g if c == 0 else gproj[m] + g
        uproj[m] = u if c == 0 else uproj[m] + u

    def expert_act(m):
        inv_rms = lax.rsqrt(squares[...] * inv_feat + EPS)

        def activate(c, carry):
            hat = cols(c, hc)
            g = gproj[m, :, hat] * inv_rms
            u = uproj[m, :, hat] * inv_rms
            gproj[m, :, hat] = g
            uproj[m, :, hat] = u
            act_a[:, hat] = (g * jax.nn.sigmoid(g) * u).astype(BF16)
            return carry

        lax.fori_loop(0, hidden // hc, activate, 0)

    def expert_down(m):
        for c in range(count):
            put_results(m, c, dot_nn(act_a[...], wd[:, piece(c)]).astype(BF16))
            start(1, m, c)

    def combine(m, c):
        gates = [stats[m, 2 + top + k] for k in range(top)]
        at = piece(c)
        arrive(1, m, c)
        mixed = jnp.zeros((toks, PIECE), F32)
        for k in range(top):
            side = ftabt[m, k] if extra else None
            part = taken(1, m, c, tabt[m, k], side).astype(BF16)
            slots[m, k, :, at] = part
            mixed = mixed + gates[k] * part.astype(F32)
        out_ref[m, :, at] = (xin[m, :, at].astype(F32) + mixed).astype(BF16)

        @pl.when(sec < sections - 1)
        def _():
            hop(out_ref, xin, 0, m, c, sec + 1).start()

    def grads_to_experts(m, c):
        gates = [stats[m, 2 + top + k] for k in range(top)]
        at = piece(c)
        take(grad_ref, cot_ref, gin, 1, m, c, sec == sections - 1, sec + 1)
        dy = gin[m, :, at].astype(F32)
        put_rows(
            m,
            c,
            [
                (tab[m, k], ftab[m, k] if extra else None, (gates[k] * dy).astype(BF16))
                for k in range(top)
            ],
        )
        start(2, m, c)
        for k in range(top):
            own = jnp.sum(dy * slots[m, k, :, at].astype(F32), axis=-1, keepdims=True)
            sums[1 + k] = own if c == 0 else sums[1 + k] + own

    def expert_hidden_grad(m, c):
        arrive(2, m, c)
        lhs[...] = unfolded(2, m, c)
        d = dot_nt(lhs[...], wd[:, piece(c)])
        dhid[...] = d if c == 0 else dhid[...] + d

    def router_grad(m):
        inv_rms = stats[m, 0]
        affinity = [stats[m, 2 + k] for k in range(top)]
        gates = [stats[m, 2 + top + k] for k in range(top)]
        aff_total = functools.reduce(jnp.add, affinity)
        dgates = [sums[1 + k] for k in range(top)]
        inner = functools.reduce(jnp.add, [d * g for d, g in zip(dgates, gates)]) / ROUTE_SCALE
        dlog = jnp.zeros((toks, experts), F32)
        along = jnp.zeros((toks, 1), F32)
        for k in range(top):
            daff = ROUTE_SCALE / aff_total * (dgates[k] - inner)
            dlogit = daff * affinity[k] * (1.0 - affinity[k])
            dlog = dlog + pick(m, k) * dlogit
            along = along + dlogit * stats[m, 2 + 2 * top + k]
        stats[m, 1] = along

        def spread(c, carry):
            at = cols(c, half)
            term = jnp.dot(
                dlog,
                router_ref[:, at].astype(F32),
                preferred_element_type=F32,
                precision=HIGHEST,
            )
            base[m, :, at] = gin[m, :, at].astype(F32) + inv_rms * gain_ref[:, at] * term
            return carry

        lax.fori_loop(0, 2, spread, 0)

    def row_copy(m, rows_src, rows_dst, peer):
        return pltpu.make_async_remote_copy(
            src_ref=row_send.at[m, rows_src],
            dst_ref=row_recv.at[m, rows_dst],
            send_sem=tssem.at[m],
            recv_sem=trsem.at[m],
            device_id=(sec, peer),
            device_id_type=MESH,
        )

    def own_row(m):
        return pltpu.make_async_copy(
            row_send.at[m, rows_of(me)], row_recv.at[m, rows_of(me)], tlsem.at[m]
        )

    def hidden_done(m):
        def activate(c, along):
            hat = cols(c, hc)
            dh = dhid[:, hat]
            g = gproj[m, :, hat]
            u = uproj[m, :, hat]
            s = jax.nn.sigmoid(g)
            a = (dh * u * s * (1.0 + g * (1.0 - s))).astype(BF16)
            b = (dh * g * s).astype(BF16)
            act_a[:, hat] = a
            act_b[:, hat] = b
            return along + jnp.sum(a.astype(F32) * g + b.astype(F32) * u, axis=-1, keepdims=True)

        along = jnp.zeros((lhs.shape[0], 1), F32)
        along = lax.fori_loop(0, hidden // hc, activate, along)
        message = jnp.broadcast_to(along[:places], row_send.shape[1:])
        if extra:
            few = jnp.broadcast_to(along[places:], (experts * extra, row_send.shape[2]))
            rest = jnp.zeros((places - experts * extra, row_send.shape[2]), F32)
            folded = jnp.dot(
                folds[1].astype(F32),
                jnp.concatenate([few, rest], axis=0),
                preferred_element_type=F32,
                precision=HIGHEST,
            )
            lanes = lax.broadcasted_iota(jnp.int32, row_send.shape[1:], 1)
            message = jnp.where(lanes == 0, message, folded)
        row_send[m] = message
        each_other(lambda peer, mate, beyond: row_copy(m, rows_of(peer), rows_of(me), peer).start())
        own_row(m).start()

    def row_sum(table, m):
        return jnp.dot(
            table.astype(F32), row_recv[m], preferred_element_type=F32, precision=HIGHEST
        )

    def expert_rows_grad(m):
        for c in range(count):
            at = piece(c)
            summed = dot_nt(act_a[...], wg[at, :]) + dot_nt(act_b[...], wu[at, :])
            put_results(m, c, summed.astype(BF16))
            start(3, m, c)

    def gather(m, c):
        inv_rms = stats[m, 0]
        at = piece(c)
        main = pair_of(tabt, m)
        side = pair_of(ftabt, m) if extra else None
        if c == 0:
            own_row(m).wait()
            row_copy(m, others, others, lax.rem(me + 1, experts)).wait()
            along = row_sum(main, m)[:, 0:1] + stats[m, 1]
            if extra:
                along = along + row_sum(side[:toks], m)[:, 1:2]
            stats[m, 1] = inv_rms * inv_rms * inv_feat * along
        arrive(3, m, c)
        dn = taken(3, m, c, main, side)
        grad_ref[m, :, at] = (
            base[m, :, at]
            + inv_rms * (gain_ref[:, at] * dn)
            - xin[m, :, at].astype(F32) * stats[m, 1]
        ).astype(BF16)

        @pl.when(sec > 0)
        def _():
            hop(grad_ref, gin, 1, m, c, sec - 1).start()

    def weave(inward, m, outward, before):
        for c in range(count + LEAD):
            if c >= LEAD:
                outward(before, c - LEAD)
            if c < count:
                inward(m, c)

    def in_turn(body, m):
        for c in range(count):
            body(m, c)

    def relay_forward(m, carry):
        relay_pass(0, m)
        relay_pass(1, m)
        return carry

    def relay_backward(m, carry):
        relay_pass(2, m)
        relay_pass(3, m)
        return carry

    make_tables()
    early = sec < sections // 2

    @pl.when(jnp.logical_not(early))
    def _():
        lax.fori_loop(0, micro, relay_forward, 0)

    for m in range(micro):
        if m == 0:
            in_turn(to_experts, m)
            gates_of(m)
            in_turn(expert_up, m)
        else:
            weave(to_experts, m, combine, m - 1)
            in_turn(expert_up, m)
        expert_act(m)
        expert_down(m)
        if m > 0:
            gates_of(m)

    @pl.when(sec == sections - 1)
    def _():
        weave(grads_to_experts, 0, combine, micro - 1)

    @pl.when(sec < sections - 1)
    def _():
        in_turn(combine, micro - 1)

        @pl.when(early)
        def _():
            lax.fori_loop(0, micro, relay_forward, 0)
            lax.fori_loop(0, micro, relay_backward, 0)

        in_turn(grads_to_experts, 0)

    for m in range(micro):
        if m == 0:
            router_grad(m)
            in_turn(expert_hidden_grad, m)
        else:
            weave(grads_to_experts, m, gather, m - 1)
            in_turn(expert_hidden_grad, m)
        hidden_done(m)
        expert_rows_grad(m)
        if m > 0:
            router_grad(m)
    in_turn(gather, micro - 1)

    @pl.when(jnp.logical_not(early))
    def _():
        lax.fori_loop(0, micro, relay_backward, 0)

    def drain(m, carry):
        @pl.when(sec < sections - 1)
        def _():
            for c in range(count):
                hop(out_ref, xin, 0, m, c, sec + 1).wait_send()

        @pl.when(sec > 0)
        def _():
            for c in range(count):
                hop(grad_ref, gin, 1, m, c, sec - 1).wait_send()

        return carry

    lax.fori_loop(0, micro, drain, 0)


def local(x0, cotangent, expert_ids, norm_gain, router, w_gate, w_up, w_down):
    sections = lax.axis_size("pipe")
    experts = lax.axis_size("expert")
    micro, toks, feat = x0.shape
    top = expert_ids.shape[3]
    cap, extra = split_of(toks * top * 5 // (4 * experts))
    fold = 16 // extra if extra else 0
    places = experts * cap
    every = places + experts * extra
    count = feat // PIECE
    room = PIECE + (PIECE // fold if extra else 0)
    relayed = sum(way != NEAR for way in roles_of(count, extra > 0))
    hidden = w_gate.shape[3]
    ids = expert_ids[0]
    flat = ids.reshape(micro, toks * top)
    order = jnp.arange(toks * top, dtype=jnp.int32)
    earlier = (order[None, :] < order[:, None])[None]
    same = flat[:, :, None] == flat[:, None, :]
    place = jnp.sum(jnp.where(jnp.logical_and(same, earlier), 1, 0), axis=2)
    seat = jnp.where(place < cap, flat * cap + place, -1)
    seat = seat.reshape(micro, toks, top).transpose(0, 2, 1)
    ids = ids.transpose(0, 2, 1)
    if extra:
        quarter = jnp.arange(fold, dtype=jnp.int32)[None, :, None] * extra
        side = (flat * cap + place - cap)[:, None, :] + quarter
        side = jnp.where((place >= cap)[:, None, :], side, -1)
        side = side.reshape(micro, fold, toks, top).transpose(0, 3, 1, 2)
        side = side.reshape(micro, top, fold * toks)
    else:
        side = seat
    vmem = pl.BlockSpec(memory_space=pltpu.VMEM)
    hbm = pl.BlockSpec(memory_space=pl.ANY)
    out_rows, grad_rows = pl.pallas_call(
        functools.partial(kernel, sections, experts, cap, extra),
        out_shape=(jax.ShapeDtypeStruct(x0.shape, BF16), jax.ShapeDtypeStruct(x0.shape, BF16)),
        in_specs=[vmem] * 9 + [hbm] * 3,
        out_specs=(vmem, vmem),
        scratch_shapes=[
            pltpu.VMEM((feat, hidden), BF16),
            pltpu.VMEM((feat, hidden), BF16),
            pltpu.VMEM((hidden, feat), BF16),
            pltpu.VMEM((micro, toks, feat), BF16),
            pltpu.VMEM((micro, toks, feat), BF16),
            pltpu.VMEM((2, micro, places, count * room), BF16),
            pltpu.VMEM((2 * micro, places, count * room), BF16),
            pltpu.VMEM((4 * micro, places, relayed * room), BF16),
            pltpu.VMEM((micro, places, 128), F32),
            pltpu.VMEM((micro, places, 128), F32),
            pltpu.VMEM((micro, every, hidden), F32),
            pltpu.VMEM((micro, every, hidden), F32),
            pltpu.VMEM((every, hidden), F32),
            pltpu.VMEM((every, hidden), BF16),
            pltpu.VMEM((every, hidden), BF16),
            pltpu.VMEM((every, PIECE), BF16),
            pltpu.VMEM((micro, top, toks, feat), BF16),
            pltpu.VMEM((micro, toks, feat), F32),
            pltpu.VMEM((micro, 2 + 3 * top, toks, 1), F32),
            pltpu.VMEM((1 + top, toks, 1), F32),
            pltpu.VMEM((toks, experts), F32),
            pltpu.VMEM((every, 1), F32),
            pltpu.VMEM((micro, top + 1, places, toks), BF16),
            pltpu.VMEM((micro, top + 1, toks, places), BF16),
            pltpu.VMEM((micro, top + 1, places, side.shape[2]), BF16),
            pltpu.VMEM((micro, top + 1, side.shape[2], places), BF16),
            pltpu.VMEM((2, places, places) if extra else (2, 16, 128), BF16),
            pltpu.SemaphoreType.DMA((3,)),
            pltpu.SemaphoreType.DMA((2, micro, count)),
            pltpu.SemaphoreType.DMA((4 * micro, count)),
            pltpu.SemaphoreType.DMA((4 * micro, count)),
            pltpu.SemaphoreType.DMA((4 * micro, count)),
            pltpu.SemaphoreType.DMA((4 * micro, relayed, experts)),
            pltpu.SemaphoreType.DMA((4 * micro, count)),
            pltpu.SemaphoreType.DMA((4 * micro, count)),
            pltpu.SemaphoreType.DMA((2, micro, count)),
            pltpu.SemaphoreType.DMA((2, micro, count)),
            pltpu.SemaphoreType.DMA((micro,)),
            pltpu.SemaphoreType.DMA((micro,)),
            pltpu.SemaphoreType.DMA((micro,)),
        ],
        compiler_params=pltpu.CompilerParams(
            collective_id=0, has_side_effects=True, vmem_limit_bytes=62 * 1024 * 1024
        ),
    )(
        x0,
        cotangent,
        norm_gain,
        router[0].T,
        seat[:, :, None, :],
        seat[:, :, :, None],
        side[:, :, None, :],
        side[:, :, :, None],
        ids[:, :, :, None],
        w_gate[0, 0],
        w_up[0, 0],
        w_down[0, 0],
    )
    return (out_rows[None], grad_rows[None])


def solution(mesh):
    placed = (
        P(None, "expert", None),
        P(None, "expert", None),
        P("pipe", None, "expert", None),
        P("pipe", None),
        P("pipe", None, None),
        P("pipe", "expert", None, None),
        P("pipe", "expert", None, None),
        P("pipe", "expert", None, None),
    )
    return jax.shard_map(
        local,
        mesh=mesh,
        in_specs=placed,
        out_specs=(P("pipe", None, "expert", None), P("pipe", None, "expert", None)),
        check_vma=False,
    )
```
